256 devices in a mesh: mesh: 32 (over x_lo, z, core), modes: 8 (over x_hi, y).
Axes of the slice: x: 4 (x_hi: 2, x_lo: 2; x = x_hi * 2 + x_lo), y: 4, z: 8, core: 2. Of those that a mesh axis runs over, the one named last changes fastest.
Arguments:
- subspace: float32 [64, 3, 32, 9216], P('modes', None, 'mesh'), may hold values from -14 to 14
- classes: int32 [32, 9216], P('mesh'), may hold values from 0 to 15
- level_density: float32 [16], replicated, may hold values from 0.05 to 1
Outputs:
- residual: float32 [64, 3, 32, 9216], P('modes', None, 'mesh')
- ritz_matrix: float32 [64, 64], replicated
The draws below stay inside these ranges and needn't reach their ends.
All inputs are finite; a program needn't handle non-finite values.
Results may differ from the reference program's by a relative error of at most 0.0003.
Values sent between devices are 32-bit elements; how exact they have to be, the bound alone decides.
No kernel may reach another device: no remote copies, remote signals or barrier semaphores. Data moves between devices by JAX's collectives and lax.ppermute only.
A program may use at most 128 MiB of HBM per device.

```python
import math
import jax
import jax.numpy as jnp
import numpy as np
from jax import lax

MODES = 64
NX = 96
NY = 96
LEVELS = 16
NZ = 32
NDOF = 884736


def draw_subspace(key, part):
    base = jax.random.fold_in(key, 17)
    key_noise, key_common, key_weight = jax.random.split(base, 3)
    array_shape = (MODES, 3, NZ, NX * NY)
    plane_index = jnp.arange(NZ, dtype=jnp.float32) / max(NZ - 1, 1)
    random_part = jax.random.truncated_normal(key_noise, -4.0, 4.0, array_shape, jnp.float32)
    common = jax.random.truncated_normal(key_common, -4.0, 4.0, (1, 3, NZ, NX * NY), jnp.float32)
    amplitude = 1.0 + 0.75 * plane_index
    mode_weight = jax.random.uniform(key_weight, (MODES, 1, 1, 1), jnp.float32, 0.3, 0.9)
    return ((random_part + mode_weight * common) * amplitude[None, None, :, None]).astype(jnp.float32)


def plant(array, rng, smallest, high):
    shape = array.shape
    spot = [jax.random.randint(jax.random.fold_in(rng, axis), (), 0, shape[axis]) for axis in range(len(shape))]
    array = array.at[tuple(spot)].set(smallest)
    longest = shape.index(max(shape))
    spot[longest] = (spot[longest] + 1) % shape[longest]
    return array.at[tuple(spot)].set(high)


def setup_inputs(seed: int = 0) -> dict:
    streams_of = jax.random.split(jax.random.key(seed), 4)
    return {
        "subspace": draw_subspace(jax.random.fold_in(streams_of[3], 71), 0),
        "classes": plant(jax.random.randint(streams_of[1], (NZ, NX * NY), 0, LEVELS), jax.random.fold_in(streams_of[1], 1), 0, LEVELS - 1).astype(jnp.int32),
        "level_density": jnp.clip(jnp.exp(jax.random.uniform(streams_of[2], (LEVELS,), jnp.float32, math.log(0.05), math.log(1.0))), 0.05, 1.0),
    }


highest = lax.Precision.HIGHEST
floor_modulus = 0.001
penalty_power = 3.0

def element_matrix():
    poisson_ratio = 0.3
    lame_first = poisson_ratio / ((1 + poisson_ratio) * (1 - 2 * poisson_ratio))
    shear_modulus = 1.0 / (2 * (1 + poisson_ratio))
    elastic = np.zeros((6, 6))
    elastic[:3, :3] = lame_first
    for normal_index in range(3):
        elastic[normal_index, normal_index] = lame_first + 2 * shear_modulus
        elastic[normal_index + 3, normal_index + 3] = shear_modulus
    corner_signs = [(1 - 2 * (corner & 1), 1 - 2 * (corner >> 1 & 1), 1 - 2 * (corner >> 2)) for corner in range(8)]
    gauss_point = 1.0 / np.sqrt(3.0)
    matrix = np.zeros((24, 24))
    for gauss_x in (-gauss_point, gauss_point):
        for gauss_y in (-gauss_point, gauss_point):
            for gauss_z in (-gauss_point, gauss_point):
                strain = np.zeros((6, 24))
                for corner in range(8):
                    sign_x, sign_y, sign_z = corner_signs[corner]
                    deriv_x = 2 * sign_x * (1 + sign_y * gauss_y) * (1 + sign_z * gauss_z) / 8
                    deriv_y = 2 * sign_y * (1 + sign_x * gauss_x) * (1 + sign_z * gauss_z) / 8
                    deriv_z = 2 * sign_z * (1 + sign_x * gauss_x) * (1 + sign_y * gauss_y) / 8
                    column = 3 * corner
                    strain[0, column] = deriv_x
                    strain[1, column + 1] = deriv_y
                    strain[2, column + 2] = deriv_z
                    strain[3, column] = deriv_y
                    strain[3, column + 1] = deriv_x
                    strain[4, column + 1] = deriv_z
                    strain[4, column + 2] = deriv_y
                    strain[5, column] = deriv_z
                    strain[5, column + 2] = deriv_x
                matrix = matrix + strain.T @ elastic @ strain / 8
    return matrix.reshape(8, 3, 8, 3)

def shift_in(plane, step_x, step_y, width_x):
    offset = step_x + step_y * width_x
    moved = plane
    if offset > 0:
        moved = jnp.pad(plane[..., :-offset], [(0, 0)] * (plane.ndim - 1) + [(offset, 0)])
    if step_x:
        column = lax.iota(jnp.int32, plane.shape[-1]) % width_x
        moved = jnp.where(column >= 1, moved, 0.0)
    return moved

def shift_out(force, step_x, step_y, width_x):
    moved = force
    if step_x:
        column = lax.iota(jnp.int32, force.shape[-1]) % width_x
        moved = jnp.where(column >= 1, moved, 0.0)
    offset = step_x + step_y * width_x
    if offset > 0:
        moved = jnp.pad(moved[..., offset:], [(0, 0)] * (force.ndim - 1) + [(0, offset)])
    return moved

def layer_forces(bottom, top, modulus_row, element, width_x):
    corners = []
    for step_z in (0, 1):
        source = top if step_z == 0 else bottom
        for step_y in (0, 1):
            for step_x in (0, 1):
                corners.append(shift_in(source, step_x, step_y, width_x))
    stacked = jnp.stack(corners, 0)
    forces = jnp.einsum('acbd,bkdn->akcn', element, stacked, precision=highest) * modulus_row
    force_top = jnp.zeros_like(top)
    force_bottom = jnp.zeros_like(bottom)
    for corner in range(8):
        moved_force = shift_out(forces[corner], corner & 1, corner >> 1 & 1, width_x)
        if corner >> 2 == 0:
            force_top = force_top + moved_force
        else:
            force_bottom = force_bottom + moved_force
    return (force_bottom, force_top)

def densities(classes, level_density):
    levels = level_density.shape[0]
    level_index = lax.iota(jnp.int32, levels).reshape(levels, 1, 1)
    matches = classes[None] == level_index
    return lax.optimization_barrier(jnp.sum(jnp.where(matches, level_density[:, None, None], 0.0), 0))

def ritz_solve(gram_stiff, gram_mass):
    lower_factor = jnp.linalg.cholesky(gram_mass)
    identity = jnp.eye(gram_mass.shape[0], dtype=jnp.float32)
    inverse = jax.scipy.linalg.solve_triangular(lower_factor, identity, lower=True)
    rotate = inverse.T
    ritz_matrix = jnp.dot(jnp.dot(inverse.astype(jnp.float32), gram_stiff.astype(jnp.float32), precision=highest, preferred_element_type=jnp.float32).astype(jnp.float32), rotate.astype(jnp.float32), precision=highest, preferred_element_type=jnp.float32)
    mixed_rotate = jnp.dot(rotate.astype(jnp.float32), ritz_matrix.astype(jnp.float32), precision=highest, preferred_element_type=jnp.float32)
    return (ritz_matrix, rotate, mixed_rotate)

def reference(subspace, classes, level_density):
    element = jnp.asarray(element_matrix(), jnp.float32)
    density = densities(classes, level_density)
    modulus = floor_modulus + (1.0 - floor_modulus) * density * density * density
    planes = jnp.moveaxis(subspace, 2, 0)
    below_planes = jnp.concatenate([jnp.zeros_like(planes[:1]), planes[:-1]], 0)

    def layer_step(carry, inputs):
        bottom, top, modulus_row = inputs
        return (carry, layer_forces(bottom, top, modulus_row, element, NX))
    unused, (force_bottom, force_top) = lax.scan(layer_step, jnp.zeros((), jnp.float32), (below_planes, planes, modulus))
    image_planes = force_top + jnp.concatenate([force_bottom[1:], jnp.zeros_like(force_bottom[:1])], 0)
    stiff_image = jnp.moveaxis(image_planes, 0, 2)
    mass_basis = subspace * density[None, None]
    gram_stiff = jnp.einsum('kczn,jczn->kj', subspace, stiff_image, precision=highest) / NDOF
    gram_mass = jnp.einsum('kczn,jczn->kj', subspace, mass_basis, precision=highest) / NDOF
    ritz_matrix, rotate, mixed_rotate = ritz_solve(gram_stiff, gram_mass)
    residual = jnp.einsum('kczn,kj->jczn', stiff_image, rotate, precision=highest) - jnp.einsum('kczn,kj->jczn', mass_basis, mixed_rotate, precision=highest)
    return (residual, ritz_matrix)
```

```python
import functools

import jax
import jax.numpy as jnp
import numpy as np
from jax import lax
from jax.experimental import pallas as pl
from jax.experimental.pallas import tpu as pltpu
from jax.sharding import Mesh
from jax.sharding import PartitionSpec as P

NX = 96
NY = 96
LANES = 128
MODES = ("modes_0", "modes_1")
MESH = ("mesh_0", "mesh_1", "mesh_2")

highest = lax.Precision.HIGHEST
floor_modulus = 0.001
VMEM = pl.BlockSpec(memory_space=pltpu.VMEM)
SMEM = pl.BlockSpec(memory_space=pltpu.SMEM)


def shifted(x, axis, by):
    size = lax.axis_size(axis)
    pairs = [(i, i + by) for i in range(size) if 0 <= i + by < size]
    return lax.ppermute(x, axis, pairs)


def element_matrix():
    poisson_ratio = 0.3
    lame_first = poisson_ratio / ((1 + poisson_ratio) * (1 - 2 * poisson_ratio))
    shear_modulus = 1.0 / (2 * (1 + poisson_ratio))
    elastic = np.zeros((6, 6))
    elastic[:3, :3] = lame_first
    for normal_index in range(3):
        elastic[normal_index, normal_index] = lame_first + 2 * shear_modulus
        elastic[normal_index + 3, normal_index + 3] = shear_modulus
    corner_signs = [
        (1 - 2 * (corner & 1), 1 - 2 * (corner >> 1 & 1), 1 - 2 * (corner >> 2))
        for corner in range(8)
    ]
    gauss_point = 1.0 / np.sqrt(3.0)
    matrix = np.zeros((24, 24))
    for gauss_x in (-gauss_point, gauss_point):
        for gauss_y in (-gauss_point, gauss_point):
            for gauss_z in (-gauss_point, gauss_point):
                strain = np.zeros((6, 24))
                for corner in range(8):
                    sign_x, sign_y, sign_z = corner_signs[corner]
                    deriv_x = 2 * sign_x * (1 + sign_y * gauss_y) * (1 + sign_z * gauss_z) / 8
                    deriv_y = 2 * sign_y * (1 + sign_x * gauss_x) * (1 + sign_z * gauss_z) / 8
                    deriv_z = 2 * sign_z * (1 + sign_x * gauss_x) * (1 + sign_y * gauss_y) / 8
                    column = 3 * corner
                    strain[0, column] = deriv_x
                    strain[1, column + 1] = deriv_y
                    strain[2, column + 2] = deriv_z
                    strain[3, column] = deriv_y
                    strain[3, column + 1] = deriv_x
                    strain[4, column + 1] = deriv_z
                    strain[4, column + 2] = deriv_y
                    strain[5, column] = deriv_z
                    strain[5, column + 2] = deriv_x
                matrix = matrix + strain.T @ elastic @ strain / 8
    return matrix.reshape(8, 3, 8, 3)


def parity_coefficients():
    signs = np.array([[(-1.0) ** bin(p & n).count("1") for n in range(8)] for p in range(8)])
    block = np.einsum("qn,ncmd,pm->qcpd", signs, element_matrix(), signs) / 64
    return tuple(
        float(np.float32(v))
        for v in (
            block[1, 0, 2, 1],
            block[1, 0, 1, 0] - block[1, 0, 2, 1],
            block[1, 1, 1, 1],
            block[3, 0, 3, 0],
            block[3, 0, 6, 2],
            block[3, 2, 5, 1],
            block[7, 0, 7, 0],
        )
    )


LAME, NORMAL, SHEAR, BEND, CROSS, TWIST, LAST = parity_coefficients()


def lane_index(rows):
    return lax.broadcasted_iota(jnp.int32, (rows, LANES), 1)


def rows_of_chunks(v0, v1, v2, lane):
    rows = (
        v0,
        jnp.where(lane < 32, pltpu.roll(v0, 32, 1), pltpu.roll(v1, 32, 1)),
        jnp.where(lane < 64, pltpu.roll(v1, 64, 1), pltpu.roll(v2, 64, 1)),
        pltpu.roll(v2, 96, 1),
    )
    return [jnp.where(lane < NX, r, 0.0) for r in rows]


def chunks_of_rows(o0, o1, o2, o3, lane):
    r1, r2, r3 = pltpu.roll(o1, 96, 1), pltpu.roll(o2, 64, 1), pltpu.roll(o3, 32, 1)
    return (
        jnp.where(lane < 96, o0, r1),
        jnp.where(lane < 64, r1, r2),
        jnp.where(lane < 32, r2, r3),
    )


def prep_kernel(x_ref, classes_ref, levels_ref, pieces_ref, density_ref, modulus_ref):
    classes = classes_ref[...]
    density = jnp.zeros(classes.shape, jnp.float32)
    for level in range(16):
        density = jnp.where(classes == level, levels_ref[level], density)
    density_ref[...] = density
    modulus_ref[...] = floor_modulus + (1.0 - floor_modulus) * density * density * density

    def piece(p, carry):
        for c in range(3):
            for q in range(9):
                pieces_ref[pl.ds(p * 216 + c * 9 + q, 8, stride=27), :] = x_ref[
                    pl.ds(c * 72 + p * 9 + q, 8, stride=216), :
                ]
        return carry

    lax.fori_loop(0, 8, piece, 0)


def layer(top, bottom):
    s = {k: top[k] + bottom[k] for k in top if k[1] != "00"}
    d = {k: top[k] - bottom[k] for k in top}
    even, odd = {}, {}
    trace = LAME * (s[0, "10"] + s[1, "01"] + d[2, "00"])
    even[0, "10"] = trace + NORMAL * s[0, "10"]
    even[1, "01"] = trace + NORMAL * s[1, "01"]
    odd[2, "00"] = trace + NORMAL * d[2, "00"]
    even[1, "10"] = even[0, "01"] = SHEAR * (s[1, "10"] + s[0, "01"])
    even[2, "10"] = odd[0, "00"] = SHEAR * (s[2, "10"] + d[0, "00"])
    even[2, "01"] = odd[1, "00"] = SHEAR * (s[2, "01"] + d[1, "00"])
    even[0, "11"] = BEND * s[0, "11"] + CROSS * d[2, "01"]
    even[1, "11"] = BEND * s[1, "11"] + CROSS * d[2, "10"]
    twist = TWIST * (s[2, "11"] + d[1, "10"] + d[0, "01"])
    even[2, "11"] = twist + TWIST * s[2, "11"]
    odd[1, "10"] = twist + TWIST * d[1, "10"]
    odd[0, "01"] = twist + TWIST * d[0, "01"]
    odd[0, "10"] = BEND * d[0, "10"] + CROSS * d[1, "01"]
    odd[1, "01"] = BEND * d[1, "01"] + CROSS * d[0, "10"]
    odd[2, "10"] = BEND * d[2, "10"] + CROSS * s[1, "11"]
    odd[2, "01"] = BEND * d[2, "01"] + CROSS * s[0, "11"]
    for c in range(3):
        odd[c, "11"] = LAST * d[c, "11"]
    return even, odd


def element_row(previous, rows, low, high):
    current, planes = [], []
    for p in range(3):
        fields = {}
        for c in range(3):
            u = rows[p][c]
            back = pltpu.roll(u, 1, 1)
            total, diff = u + back, u - back
            old_total, old_diff = previous[p * 3 + c]
            fields[c, "00"] = total + old_total
            fields[c, "10"] = diff + old_diff
            fields[c, "01"] = total - old_total
            fields[c, "11"] = diff - old_diff
            current.append((total, diff))
        planes.append(fields)
    own, below, above = planes
    even, odd = layer(own, below)
    even_up, odd_up = layer(above, own)
    plus, minus = [], []
    for c in range(3):
        f = {}
        for k in ("00", "10", "01", "11"):
            if k == "00":
                f[k] = low * odd[c, k] - high * odd_up[c, k]
            else:
                f[k] = low * (even[c, k] + odd[c, k]) + high * (even_up[c, k] - odd_up[c, k])
        plus.append((f["00"] + f["01"], f["10"] + f["11"]))
        minus.append((f["00"] - f["01"], f["10"] - f["11"]))
    return current, plus, minus


def stiffness_kernel(own, below, above, modulus, modulus_up, out, low_rows, high_rows):
    wide = lane_index(24)
    for source, target in ((modulus, low_rows), (modulus_up, high_rows)):
        chunks = [source[pl.ds(k, 24, stride=3), :] for k in range(3)]
        for k, row in enumerate(rows_of_chunks(*chunks, wide)):
            target[pl.ds(k, 24, stride=4), :] = row
        target[pl.ds(NY, 8), :] = jnp.zeros((8, LANES), jnp.float32)
    lane = lane_index(8)
    planes = (own, below, above)

    def chunk(plane, c, index):
        return plane[pl.ds(c * 72 + index, 8, stride=216), :]

    def moduli(j):
        return tuple(
            jnp.broadcast_to(ref[pl.ds(j, 1), :], (8, LANES)) for ref in (low_rows, high_rows)
        )

    zero = jnp.zeros((8, LANES), jnp.float32)
    first = [[jnp.where(lane < NX, chunk(plane, c, 0), 0.0) for c in range(3)] for plane in planes]
    state, plus, unused = element_row([(zero, zero)] * 9, first, *moduli(0))

    def group(g, carry):
        state, plus = carry
        rows = [[None] * 3 for unused in range(3)]
        for p in range(3):
            for c in range(3):
                v0, v1, v2 = [chunk(planes[p], c, 3 * g + k) for k in range(3)]
                v3 = chunk(planes[p], c, jnp.minimum(3 * g + 3, 71))
                rows[p][c] = rows_of_chunks(v0, v1, v2, lane)[1:] + [jnp.where(lane < NX, v3, 0.0)]
        results = [[] for unused in range(3)]
        for step in range(4):
            here = [[rows[p][c][step] for c in range(3)] for p in range(3)]
            state, new_plus, minus = element_row(state, here, *moduli(4 * g + 1 + step))
            for c in range(3):
                even, odd = plus[c][0] + minus[c][0], plus[c][1] + minus[c][1]
                results[c].append((even + odd) + pltpu.roll(even - odd, LANES - 1, 1))
            plus = new_plus
        base = (g // 3) * 216 + (g % 3) * 3
        for c in range(3):
            for k, v in enumerate(chunks_of_rows(*results[c], lane)):
                out[pl.ds(base + c * 9 + k, 8, stride=27), :] = v
        return state, plus

    lax.fori_loop(0, 24, group, (state, plus))


def gram_kernel(basis, image, density, out):
    acc = jnp.zeros((64, LANES), jnp.float32)
    for c in range(3):
        for q in range(9):
            t = c * 9 + q
            b = basis[pl.ds(t, 64, stride=27), :]
            v = image[pl.ds(t, 64, stride=27), :]
            m = b * density[pl.ds(q, 1), :]
            both = jnp.concatenate([v, m], 0)
            acc = acc + lax.dot_general(
                b, both, (((1,), (1,)), ((), ())), precision=highest, preferred_element_type=jnp.float32
            )
    out[...] = acc


def dot(a, b, dims):
    return lax.dot_general(
        a, b, (dims, ((), ())), precision=highest, preferred_element_type=jnp.float32
    )


def inverse_factor(mass):
    row = lax.broadcasted_iota(jnp.int32, (64, LANES), 0)
    lane = lax.broadcasted_iota(jnp.int32, (64, LANES), 1)
    w = jnp.where(lane < 64, mass, jnp.where(lane - 64 == row, 1.0, 0.0))
    for k in range(0, 64, 2):
        r0, r1 = w[k : k + 1, :], w[k + 1 : k + 2, :]
        c0, c1 = w[:, k : k + 1], w[:, k + 1 : k + 2]
        a, b, d = r0[:, k : k + 1], r0[:, k + 1 : k + 2], r1[:, k + 1 : k + 2]
        inv = 1.0 / (a * d - b * b)
        x0 = (d * r0 - b * r1) * inv
        x1 = (a * r1 - b * r0) * inv
        w = jnp.where(row > k + 1, w - c0 * x0 - c1 * x1, w)
    diagonal = jnp.sum(jnp.where(lane == row, w, 0.0), 1, keepdims=True)
    left = jnp.sum(jnp.where(lane == row - 1, w, 0.0), 1, keepdims=True)
    odd = row % 2 == 1
    up = pltpu.roll(w, 1, 0)
    up_diagonal = pltpu.roll(jnp.broadcast_to(diagonal, (64, LANES)), 1, 0)
    ratio = jnp.where(odd, left / jnp.where(odd, up_diagonal, 1.0), 0.0)
    pivot = diagonal - ratio * left
    scaled = (w - ratio * up) * lax.rsqrt(pivot)
    return scaled[:, 64:]


def residual_kernel(total_dofs, gram, basis, image, density, out, ritz_ref):
    scale = 1.0 / total_dofs
    both = gram[...] * scale
    mass = pltpu.roll(both, 64, 1)
    inverse = inverse_factor(mass)
    stiff = both[:, :64]
    ritz = dot(dot(inverse, stiff, ((1,), (0,))), inverse, ((1,), (1,)))
    ritz_ref[...] = ritz
    mixed = dot(ritz, inverse, ((0,), (0,)))
    weights = jnp.concatenate([inverse, -mixed], 1)
    for c in range(3):
        for q in range(9):
            t = c * 9 + q
            b = basis[pl.ds(t, 64, stride=27), :]
            v = image[pl.ds(t, 64, stride=27), :]
            m = b * density[pl.ds(q, 1), :]
            out[pl.ds(t, 64, stride=27), :] = dot(
                weights, jnp.concatenate([v, m], 0), ((1,), (0,))
            )


def join_kernel(x_ref, out_ref):
    def piece(p, carry):
        for c in range(3):
            for q in range(9):
                out_ref[pl.ds(c * 72 + p * 9 + q, 8, stride=216), :] = x_ref[
                    pl.ds(p * 216 + c * 9 + q, 8, stride=27), :
                ]
        return carry

    lax.fori_loop(0, 8, piece, 0)


def room(mib):
    return pltpu.CompilerParams(vmem_limit_bytes=mib << 20)


def f32(*shape):
    return jax.ShapeDtypeStruct(shape, jnp.float32)


def exchanged(x, axis, mask):
    size = lax.axis_size(axis)
    return lax.ppermute(x, axis, [(i, i ^ mask) for i in range(size)])


def total_sum(x):
    for axis in ("modes_1", ("mesh_0", "modes_0")):
        x = (x + exchanged(x, axis, 1)) + (exchanged(x, axis, 2) + exchanged(x, axis, 3))
    x = x + exchanged(x, "mesh_2", 1)
    for mask in (1, 2, 4):
        x = x + exchanged(x, "mesh_1", mask)
    return x


def per_device(subspace, classes, level_density):
    total_dofs = 3 * NX * NY * subspace.shape[2] * lax.axis_size(MESH)
    flat = subspace.reshape(1728, LANES)
    below = shifted(flat, MESH, 1)
    above = shifted(flat, MESH, -1)
    pieces, density, modulus = pl.pallas_call(
        prep_kernel,
        in_specs=[VMEM, VMEM, SMEM],
        out_specs=[VMEM, VMEM, VMEM],
        out_shape=[f32(1728, LANES), f32(72, LANES), f32(72, LANES)],
        cost_estimate=pl.CostEstimate(flops=10**5, bytes_accessed=1_800_000, transcendentals=0),
        compiler_params=room(8),
        name="prep",
    )(flat, classes.reshape(72, LANES), level_density)
    modulus_up = shifted(modulus, MESH, -1)

    def all_to_all(x):
        x = x.reshape(8, 216, LANES)
        return lax.all_to_all(x, MODES, split_axis=0, concat_axis=0, tiled=True).reshape(1728, LANES)

    basis = all_to_all(pieces)
    image_pieces = pl.pallas_call(
        stiffness_kernel,
        in_specs=[VMEM] * 5,
        out_specs=VMEM,
        out_shape=f32(1728, LANES),
        scratch_shapes=[pltpu.VMEM((104, LANES), jnp.float32)] * 2,
        cost_estimate=pl.CostEstimate(
            flops=27_000_000, bytes_accessed=3_600_000, transcendentals=0
        ),
        compiler_params=room(12),
        name="stiffness",
    )(flat, below, above, modulus, modulus_up)
    image = all_to_all(image_pieces)
    band = lax.axis_index(MODES)
    band_density = lax.dynamic_slice_in_dim(density, band * 9, 9, 0)
    local = pl.pallas_call(
        gram_kernel,
        in_specs=[VMEM] * 3,
        out_specs=VMEM,
        out_shape=f32(64, LANES),
        compiler_params=room(8),
        name="grams",
    )(basis, image, band_density)
    gram = total_sum(local)
    residual_pieces, ritz_matrix = pl.pallas_call(
        functools.partial(residual_kernel, total_dofs),
        in_specs=[VMEM] * 4,
        out_specs=[VMEM, VMEM],
        out_shape=[f32(1728, LANES), f32(64, 64)],
        compiler_params=room(12),
        name="residual",
    )(gram, basis, image, band_density)
    joined = pl.pallas_call(
        join_kernel,
        in_specs=[VMEM],
        out_specs=VMEM,
        out_shape=f32(1728, LANES),
        compiler_params=room(8),
        name="join",
    )(all_to_all(residual_pieces))
    return (joined.reshape(subspace.shape), ritz_matrix)


def solution(mesh):
    split = Mesh(
        mesh.devices.reshape(2, 8, 2, 2, 4), ("mesh_0", "mesh_1", "mesh_2", "modes_0", "modes_1")
    )
    placed = (P(MODES, None, MESH, None), P(MESH, None), P())
    return jax.shard_map(
        per_device,
        mesh=split,
        in_specs=placed,
        out_specs=(P(MODES, None, MESH, None), P()),
        check_vma=False,
    )
```

```python
import functools

import jax
import jax.numpy as jnp
import numpy as np
from jax import lax
from jax.experimental import pallas as pl
from jax.experimental.pallas import tpu as pltpu
from jax.sharding import Mesh
from jax.sharding import PartitionSpec as P


NX = 96
NY = 96
LANES = 128
MODES = ("modes_0", "modes_1")
MESH = ("mesh_0", "mesh_1", "mesh_2")

highest = lax.Precision.HIGHEST
floor_modulus = 0.001
VMEM = pl.BlockSpec(memory_space=pltpu.VMEM)
SMEM = pl.BlockSpec(memory_space=pltpu.SMEM)
HBM = pl.BlockSpec(memory_space=pltpu.HBM)


def shifted(x, axis, by):
    size = lax.axis_size(axis)
    pairs = [(i, i + by) for i in range(size) if 0 <= i + by < size]
    return lax.ppermute(x, axis, pairs)


def element_matrix():
    poisson_ratio = 0.3
    lame_first = poisson_ratio / ((1 + poisson_ratio) * (1 - 2 * poisson_ratio))
    shear_modulus = 1.0 / (2 * (1 + poisson_ratio))
    elastic = np.zeros((6, 6))
    elastic[:3, :3] = lame_first
    for normal_index in range(3):
        elastic[normal_index, normal_index] = lame_first + 2 * shear_modulus
        elastic[normal_index + 3, normal_index + 3] = shear_modulus
    corner_signs = [
        (1 - 2 * (corner & 1), 1 - 2 * (corner >> 1 & 1), 1 - 2 * (corner >> 2))
        for corner in range(8)
    ]
    gauss_point = 1.0 / np.sqrt(3.0)
    matrix = np.zeros((24, 24))
    for gauss_x in (-gauss_point, gauss_point):
        for gauss_y in (-gauss_point, gauss_point):
            for gauss_z in (-gauss_point, gauss_point):
                strain = np.zeros((6, 24))
                for corner in range(8):
                    sign_x, sign_y, sign_z = corner_signs[corner]
                    deriv_x = 2 * sign_x * (1 + sign_y * gauss_y) * (1 + sign_z * gauss_z) / 8
                    deriv_y = 2 * sign_y * (1 + sign_x * gauss_x) * (1 + sign_z * gauss_z) / 8
                    deriv_z = 2 * sign_z * (1 + sign_x * gauss_x) * (1 + sign_y * gauss_y) / 8
                    column = 3 * corner
                    strain[0, column] = deriv_x
                    strain[1, column + 1] = deriv_y
                    strain[2, column + 2] = deriv_z
                    strain[3, column] = deriv_y
                    strain[3, column + 1] = deriv_x
                    strain[4, column + 1] = deriv_z
                    strain[4, column + 2] = deriv_y
                    strain[5, column] = deriv_z
                    strain[5, column + 2] = deriv_x
                matrix = matrix + strain.T @ elastic @ strain / 8
    return matrix.reshape(8, 3, 8, 3)


def parity_coefficients():
    signs = np.array([[(-1.0) ** bin(p & n).count("1") for n in range(8)] for p in range(8)])
    block = np.einsum("qn,ncmd,pm->qcpd", signs, element_matrix(), signs) / 64
    unit = block[3, 0, 6, 2]
    ratios = tuple(
        float(np.float32(v / unit))
        for v in (
            block[1, 0, 2, 1],
            block[1, 0, 1, 0] - block[1, 0, 2, 1],
            block[1, 1, 1, 1],
            block[3, 0, 3, 0],
            block[3, 2, 5, 1],
            block[7, 0, 7, 0],
        )
    )
    return (float(np.float32(unit)), *ratios)


UNIT, LAME, NORMAL, SHEAR, BEND, TWIST, LAST = parity_coefficients()


def lane_index(rows):
    return lax.broadcasted_iota(jnp.int32, (rows, LANES), 1)


def modulus_of(density):
    return floor_modulus + (1.0 - floor_modulus) * density * density * density


def densities(classes, levels):
    density = jnp.zeros(classes.shape, jnp.float32)
    for level in range(16):
        density = jnp.where(classes == level, levels[level], density)
    return density


def split_kernel(x_hbm, pieces_hbm, x_ref, pieces_ref, load, store):
    loads = [
        pltpu.make_async_copy(x_hbm.at[:, c], x_ref.at[c], load.at[c]) for c in range(3)
    ]
    for copy in loads:
        copy.start()
    stores = []
    for c in range(3):
        loads[c].wait()
        for p in range(8):
            for q in range(9):
                pieces_ref[pl.ds(p * 216 + c * 9 + q, 8, stride=27), :] = x_ref[
                    c, :, p * 9 + q, :
                ]
            if c == 2:
                part = pl.ds(p * 216, 216)
                stores.append(
                    pltpu.make_async_copy(pieces_ref.at[part], pieces_hbm.at[part], store.at[p])
                )
                stores[-1].start()
    for copy in stores:
        copy.wait()


def layer(top, bottom):
    s = {k: top[k] + bottom[k] for k in top if k[1] != "00"}
    d = {k: top[k] - bottom[k] for k in top}
    even, odd = {}, {}
    trace = LAME * (s[0, "10"] + s[1, "01"] + d[2, "00"])
    even[0, "10"] = trace + NORMAL * s[0, "10"]
    even[1, "01"] = trace + NORMAL * s[1, "01"]
    odd[2, "00"] = trace + NORMAL * d[2, "00"]
    even[1, "10"] = even[0, "01"] = SHEAR * (s[1, "10"] + s[0, "01"])
    even[2, "10"] = odd[0, "00"] = SHEAR * (s[2, "10"] + d[0, "00"])
    even[2, "01"] = odd[1, "00"] = SHEAR * (s[2, "01"] + d[1, "00"])
    even[0, "11"] = BEND * s[0, "11"] + d[2, "01"]
    even[1, "11"] = BEND * s[1, "11"] + d[2, "10"]
    twist = s[2, "11"] + d[1, "10"] + d[0, "01"]
    even[2, "11"] = TWIST * (twist + s[2, "11"])
    odd[1, "10"] = TWIST * (twist + d[1, "10"])
    odd[0, "01"] = TWIST * (twist + d[0, "01"])
    odd[0, "10"] = BEND * d[0, "10"] + d[1, "01"]
    odd[1, "01"] = BEND * d[1, "01"] + d[0, "10"]
    odd[2, "10"] = BEND * d[2, "10"] + s[1, "11"]
    odd[2, "01"] = BEND * d[2, "01"] + s[0, "11"]
    for c in range(3):
        odd[c, "11"] = LAST * d[c, "11"]
    return even, odd


PARITIES = ("00", "10", "01", "11")


def stiffness_kernel(
    own, below, above, classes, classes_up, levels, out, low, high, even_buf, odd_buf, sums, ends
):
    low[...] = UNIT * modulus_of(densities(classes[...], levels))
    is_top = lax.axis_index(MESH) == lax.axis_size(MESH) - 1
    high[...] = modulus_of(densities(classes_up[...], levels)) * jnp.where(is_top, 0.0, UNIT)
    lane = lane_index(8)
    inside = ((lane != 0) & (lane != 96), lane != 64, lane != 32)
    before_end = (lane != 95, lane != 63, (lane != 31) & (lane != 127))
    planes = (own, below, above)

    def forward(g, buf):
        for p in range(3):
            for c in range(3):
                s = p * 3 + c
                old = sums[2 * s], sums[2 * s + 1]
                runs = [planes[p][pl.ds(c * 72 + 3 * g + k, 8, stride=216), :] for k in range(3)]
                rolled = [pltpu.roll(u, 1, 1) for u in runs]
                for k in range(3):
                    back = jnp.where(inside[k], rolled[k], 0.0)
                    if k:
                        back = jnp.where(lane == 0, rolled[k - 1], back)
                    total, diff = runs[k] + back, runs[k] - back
                    new = pltpu.roll(total, 96, 1), pltpu.roll(diff, 96, 1)
                    row_total = jnp.where(lane < 96, old[0], new[0])
                    row_diff = jnp.where(lane < 96, old[1], new[1])
                    old = new
                    base = k * 36 + s * 4
                    buf[base] = total + row_total
                    buf[base + 1] = diff + row_diff
                    buf[base + 2] = total - row_total
                    buf[base + 3] = diff - row_diff
                sums[2 * s], sums[2 * s + 1] = old

    def store(run, c, value):
        row = lax.div(run, 9) * 216 + lax.rem(run, 9) + c * 9
        out[pl.ds(row, 8, stride=27), :] = value

    def inverse(g, buf):
        kept, moved = [], []
        for k in range(3):
            own_f, below_f, above_f = [
                {
                    (c, name): buf[k * 36 + (p * 3 + c) * 4 + n]
                    for c in range(3)
                    for n, name in enumerate(PARITIES)
                }
                for p in range(3)
            ]
            even, odd = layer(own_f, below_f)
            even_up, odd_up = layer(above_f, own_f)
            weight = jnp.broadcast_to(low[pl.ds(3 * g + k, 1), :], (8, LANES))
            weight_up = jnp.broadcast_to(high[pl.ds(3 * g + k, 1), :], (8, LANES))
            keep, move = [], []
            for c in range(3):
                f = {"00": weight * odd[c, "00"] - weight_up * odd_up[c, "00"]}
                for n in PARITIES[1:]:
                    f[n] = weight * (even[c, n] + odd[c, n]) + weight_up * (
                        even_up[c, n] - odd_up[c, n]
                    )
                keep.append((f["00"] + f["10"], f["01"] + f["11"]))
                move.append(
                    [pltpu.roll(v, 127, 1) for v in (f["00"] - f["10"], f["01"] - f["11"])]
                )
            kept.append(keep)
            moved.append(move)
        for c in range(3):
            old_plus, old_minus = ends[2 * c], ends[2 * c + 1]
            for k in range(3):
                pair = []
                for y in range(2):
                    from_right = jnp.where(before_end[k], moved[k][c][y], 0.0)
                    if k < 2:
                        from_right = jnp.where(lane == 127, moved[k + 1][c][y], from_right)
                    pair.append(kept[k][c][y] + from_right)
                plus, minus = pair[0] + pair[1], pltpu.roll(pair[0] - pair[1], 32, 1)
                store(
                    jnp.maximum(3 * g + k - 1, 0),
                    c,
                    old_plus + jnp.where(lane < 32, old_minus, minus),
                )
                old_plus, old_minus = plus, minus
            ends[2 * c], ends[2 * c + 1] = old_plus, old_minus

    zero = jnp.zeros((8, LANES), jnp.float32)
    for k in range(18):
        sums[k] = zero
    for k in range(6):
        ends[k] = zero
    forward(0, even_buf)

    def two_groups(h, carry):
        forward(2 * h + 1, odd_buf)
        inverse(2 * h, even_buf)
        forward(jnp.minimum(2 * h + 2, 23), even_buf)
        inverse(2 * h + 1, odd_buf)
        return carry

    lax.fori_loop(0, 12, two_groups, 0)
    for c in range(3):
        store(71, c, ends[2 * c] + jnp.where(lane < 32, ends[2 * c + 1], 0.0))


def mass_kernel(basis, classes, levels, mass, band_density, density):
    density[...] = densities(classes[...], levels)
    band = lax.axis_index(MODES)
    acc = jnp.zeros((64, 64), jnp.float32)
    for q in range(9):
        row = density[pl.ds(band * 9 + q, 1), :]
        band_density[pl.ds(q, 1), :] = row
        for c in range(3):
            b = basis[pl.ds(c * 9 + q, 64, stride=27), :]
            acc = acc + dot(b, b * row, ((1,), (1,)))
    mass[...] = acc


def square_index():
    row = lax.broadcasted_iota(jnp.int32, (64, 64), 0)
    return row, lax.broadcasted_iota(jnp.int32, (64, 64), 1)


def gram_kernel(basis, image, mass, out):
    acc = jnp.zeros((64, 64), jnp.float32)
    for t in range(27):
        b = basis[pl.ds(t, 64, stride=27), :]
        v = image[pl.ds(t, 64, stride=27), :]
        acc = acc + dot(b, v, ((1,), (1,)))
    row, column = square_index()
    mass = mass[...]
    packed = jnp.where(row >= column, acc, mass)
    diagonal = jnp.sum(jnp.where(row == column, mass, 0.0), 0, keepdims=True)
    top = jnp.concatenate([packed[:32], packed[32:]], 1)
    last = jnp.broadcast_to(jnp.concatenate([diagonal, diagonal], 1), (8, LANES))
    block = jnp.concatenate([top, last], 0)
    for k in range(16):
        out[k] = block


def unpacked(block):
    row, column = square_index()
    packed = jnp.concatenate([block[:32, :64], block[:32, 64:]], 0)
    other = jnp.transpose(packed)
    diagonal = jnp.broadcast_to(block[32:33, :64], (64, 64))
    stiff = jnp.where(row >= column, packed, other)
    mass = jnp.where(row == column, diagonal, jnp.where(row < column, packed, other))
    return stiff, mass


def dot(a, b, dims):
    return lax.dot_general(
        a, b, (dims, ((), ())), precision=highest, preferred_element_type=jnp.float32
    )


def inverse_factor(mass):
    row = lax.broadcasted_iota(jnp.int32, (64, LANES), 0)
    lane = lax.broadcasted_iota(jnp.int32, (64, LANES), 1)
    w = jnp.where(
        lane < 64,
        jnp.concatenate([mass, mass], 1),
        jnp.where(lane - 64 == row, 1.0, 0.0),
    )
    for k in range(0, 64, 2):
        r0, r1 = w[k : k + 1, :], w[k + 1 : k + 2, :]
        c0, c1 = w[:, k : k + 1], w[:, k + 1 : k + 2]
        a, b, d = r0[:, k : k + 1], r0[:, k + 1 : k + 2], r1[:, k + 1 : k + 2]
        inv = 1.0 / (a * d - b * b)
        x0 = (d * r0 - b * r1) * inv
        x1 = (a * r1 - b * r0) * inv
        w = jnp.where(row > k + 1, w - c0 * x0 - c1 * x1, w)
    diagonal = jnp.sum(jnp.where(lane == row, w, 0.0), 1, keepdims=True)
    left = jnp.sum(jnp.where(lane == row - 1, w, 0.0), 1, keepdims=True)
    odd = row % 2 == 1
    up = pltpu.roll(w, 1, 0)
    up_diagonal = pltpu.roll(jnp.broadcast_to(diagonal, (64, LANES)), 1, 0)
    ratio = jnp.where(odd, left / jnp.where(odd, up_diagonal, 1.0), 0.0)
    pivot = diagonal - ratio * left
    scaled = (w - ratio * up) * lax.rsqrt(pivot)
    return scaled[:, 64:]


def residual_kernel(total_dofs, gram, basis, image, density, out, ritz_ref):
    scale = 1.0 / total_dofs
    stiff, mass = unpacked(gram[...] * scale)
    inverse = inverse_factor(mass)
    ritz = dot(dot(inverse, stiff, ((1,), (0,))), inverse, ((1,), (1,)))
    ritz_ref[...] = ritz
    mixed = dot(ritz, inverse, ((0,), (0,)))
    weights = jnp.concatenate([inverse, -mixed], 1)
    for c in range(3):
        for q in range(9):
            t = c * 9 + q
            b = basis[pl.ds(t, 64, stride=27), :]
            v = image[pl.ds(t, 64, stride=27), :]
            m = b * density[pl.ds(q, 1), :]
            out[pl.ds(t, 64, stride=27), :] = dot(
                weights, jnp.concatenate([v, m], 0), ((1,), (0,))
            )


def join_kernel(x_ref, out_ref):
    def piece(p, carry):
        for c in range(3):
            for q in range(9):
                out_ref[pl.ds(c * 72 + p * 9 + q, 8, stride=216), :] = x_ref[
                    pl.ds(p * 216 + c * 9 + q, 8, stride=27), :
                ]
        return carry

    lax.fori_loop(0, 8, piece, 0)


def room(mib):
    return pltpu.CompilerParams(vmem_limit_bytes=mib << 20)


def f32(*shape):
    return jax.ShapeDtypeStruct(shape, jnp.float32)


def total_sum(x):
    layer_axes = ("mesh_0", "modes_0", "modes_1")
    x = jnp.sum(lax.all_to_all(x, layer_axes, split_axis=0, concat_axis=0, tiled=True), 0)
    x = x + lax.ppermute(x, "mesh_2", [(0, 1), (1, 0)])
    x = jnp.broadcast_to(x[None], (8, *x.shape))
    return jnp.sum(lax.all_to_all(x, "mesh_1", split_axis=0, concat_axis=0, tiled=True), 0)


def per_device(subspace, classes, level_density):
    total_dofs = 3 * NX * NY * subspace.shape[2] * lax.axis_size(MESH)
    flat = subspace.reshape(1728, LANES)
    classes = classes.reshape(72, LANES)
    below = shifted(flat, MESH, 1)
    above = shifted(flat, MESH, -1)
    classes_up = shifted(classes, MESH, -1)
    split = pl.pallas_call(
        split_kernel,
        in_specs=[HBM],
        out_specs=HBM,
        out_shape=f32(1728, LANES),
        scratch_shapes=[
            pltpu.VMEM((3, 8, 72, LANES), jnp.float32),
            pltpu.VMEM((1728, LANES), jnp.float32),
            pltpu.SemaphoreType.DMA((3,)),
            pltpu.SemaphoreType.DMA((8,)),
        ],
        compiler_params=room(4),
        cost_estimate=pl.CostEstimate(flops=10**5, bytes_accessed=1_800_000, transcendentals=0),
        name="split",
    )
    pieces = split(pltpu.with_memory_space_constraint(flat.reshape(8, 3, 72, LANES), pltpu.HBM))

    def all_to_all(x):
        x = x.reshape(8, 216, LANES)
        return lax.all_to_all(x, MODES, split_axis=0, concat_axis=0, tiled=True).reshape(1728, LANES)

    basis = all_to_all(pieces)
    image_pieces = pl.pallas_call(
        stiffness_kernel,
        in_specs=[VMEM] * 5 + [SMEM],
        out_specs=VMEM,
        out_shape=f32(1728, LANES),
        scratch_shapes=[pltpu.VMEM((72, LANES), jnp.float32)] * 2
        + [pltpu.VMEM((n, 8, LANES), jnp.float32) for n in (108, 108, 18, 6)],
        compiler_params=room(12),
        cost_estimate=pl.CostEstimate(
            flops=27_000_000, bytes_accessed=3_600_000, transcendentals=0
        ),
        name="stiffness",
    )(flat, below, above, classes, classes_up, level_density)
    image = all_to_all(image_pieces)
    mass, band_density = pl.pallas_call(
        mass_kernel,
        in_specs=[VMEM, VMEM, SMEM],
        out_specs=[VMEM, VMEM],
        out_shape=[f32(64, 64), f32(16, LANES)],
        scratch_shapes=[pltpu.VMEM((72, LANES), jnp.float32)],
        compiler_params=room(8),
        cost_estimate=pl.CostEstimate(flops=10**8, bytes_accessed=900_000, transcendentals=0),
        name="mass",
    )(basis, classes, level_density)
    local = pl.pallas_call(
        gram_kernel,
        in_specs=[VMEM] * 3,
        out_specs=VMEM,
        out_shape=f32(16, 40, LANES),
        compiler_params=room(8),
        name="grams",
    )(basis, image, mass)
    gram = total_sum(local)
    residual_pieces, ritz_matrix = pl.pallas_call(
        functools.partial(residual_kernel, total_dofs),
        in_specs=[VMEM] * 4,
        out_specs=[VMEM, VMEM],
        out_shape=[f32(1728, LANES), f32(64, 64)],
        compiler_params=room(12),
        name="residual",
    )(gram, basis, image, band_density)
    joined = pl.pallas_call(
        join_kernel,
        in_specs=[VMEM],
        out_specs=VMEM,
        out_shape=f32(1728, LANES),
        compiler_params=room(8),
        name="join",
    )(all_to_all(residual_pieces))
    return (joined.reshape(subspace.shape), ritz_matrix)


def solution(mesh):
    split = Mesh(
        mesh.devices.reshape(2, 8, 2, 2, 4), ("mesh_0", "mesh_1", "mesh_2", "modes_0", "modes_1")
    )
    placed = (P(MODES, None, MESH, None), P(MESH, None), P())
    return jax.shard_map(
        per_device,
        mesh=split,
        in_specs=placed,
        out_specs=(P(MODES, None, MESH, None), P()),
        check_vma=False,
    )
```

```python
import functools

import jax
import jax.numpy as jnp
import numpy as np
from jax import lax
from jax.experimental import pallas as pl
from jax.experimental.pallas import tpu as pltpu
from jax.sharding import Mesh
from jax.sharding import PartitionSpec as P


NX = 96
NY = 96
LANES = 128
MODES = ("modes_0", "modes_1")
MESH = ("mesh_0", "mesh_1", "mesh_2")

highest = lax.Precision.HIGHEST
floor_modulus = 0.001
AHEAD = 2
VMEM = pl.BlockSpec(memory_space=pltpu.VMEM)
SMEM = pl.BlockSpec(memory_space=pltpu.SMEM)
HBM = pl.BlockSpec(memory_space=pltpu.HBM)


def shifted(x, axis, by):
    size = lax.axis_size(axis)
    pairs = [(i, i + by) for i in range(size) if 0 <= i + by < size]
    return lax.ppermute(x, axis, pairs)


def element_matrix():
    poisson_ratio = 0.3
    lame_first = poisson_ratio / ((1 + poisson_ratio) * (1 - 2 * poisson_ratio))
    shear_modulus = 1.0 / (2 * (1 + poisson_ratio))
    elastic = np.zeros((6, 6))
    elastic[:3, :3] = lame_first
    for normal_index in range(3):
        elastic[normal_index, normal_index] = lame_first + 2 * shear_modulus
        elastic[normal_index + 3, normal_index + 3] = shear_modulus
    corner_signs = [
        (1 - 2 * (corner & 1), 1 - 2 * (corner >> 1 & 1), 1 - 2 * (corner >> 2))
        for corner in range(8)
    ]
    gauss_point = 1.0 / np.sqrt(3.0)
    matrix = np.zeros((24, 24))
    for gauss_x in (-gauss_point, gauss_point):
        for gauss_y in (-gauss_point, gauss_point):
            for gauss_z in (-gauss_point, gauss_point):
                strain = np.zeros((6, 24))
                for corner in range(8):
                    sign_x, sign_y, sign_z = corner_signs[corner]
                    deriv_x = 2 * sign_x * (1 + sign_y * gauss_y) * (1 + sign_z * gauss_z) / 8
                    deriv_y = 2 * sign_y * (1 + sign_x * gauss_x) * (1 + sign_z * gauss_z) / 8
                    deriv_z = 2 * sign_z * (1 + sign_x * gauss_x) * (1 + sign_y * gauss_y) / 8
                    column = 3 * corner
                    strain[0, column] = deriv_x
                    strain[1, column + 1] = deriv_y
                    strain[2, column + 2] = deriv_z
                    strain[3, column] = deriv_y
                    strain[3, column + 1] = deriv_x
                    strain[4, column + 1] = deriv_z
                    strain[4, column + 2] = deriv_y
                    strain[5, column] = deriv_z
                    strain[5, column + 2] = deriv_x
                matrix = matrix + strain.T @ elastic @ strain / 8
    return matrix.reshape(8, 3, 8, 3)


def parity_coefficients():
    signs = np.array([[(-1.0) ** bin(p & n).count("1") for n in range(8)] for p in range(8)])
    block = np.einsum("qn,ncmd,pm->qcpd", signs, element_matrix(), signs) / 64
    unit = block[3, 0, 6, 2]
    ratios = tuple(
        float(np.float32(v / unit))
        for v in (
            block[1, 0, 2, 1],
            block[1, 0, 1, 0] - block[1, 0, 2, 1],
            block[1, 1, 1, 1],
            block[3, 0, 3, 0],
            block[3, 2, 5, 1],
            block[7, 0, 7, 0],
        )
    )
    return (float(np.float32(unit)), *ratios)


UNIT, LAME, NORMAL, SHEAR, BEND, TWIST, LAST = parity_coefficients()


def lane_index(rows):
    return lax.broadcasted_iota(jnp.int32, (rows, LANES), 1)


def modulus_of(density):
    return floor_modulus + (1.0 - floor_modulus) * density * density * density


def densities(classes, levels):
    density = jnp.zeros(classes.shape, jnp.float32)
    for level in range(16):
        density = jnp.where(classes == level, levels[level], density)
    return density


def split_kernel(x_hbm, pieces_hbm, x_ref, pieces_ref, load, store):
    loads = [
        pltpu.make_async_copy(x_hbm.at[:, c], x_ref.at[c], load.at[c]) for c in range(3)
    ]
    for copy in loads:
        copy.start()
    stores = []
    for c in range(3):
        loads[c].wait()
        for p in range(8):
            for q in range(9):
                pieces_ref[pl.ds(p * 216 + c * 9 + q, 8, stride=27), :] = x_ref[
                    c, :, p * 9 + q, :
                ]
            if c == 2:
                part = pl.ds(p * 216, 216)
                stores.append(
                    pltpu.make_async_copy(pieces_ref.at[part], pieces_hbm.at[part], store.at[p])
                )
                stores[-1].start()
    for copy in stores:
        copy.wait()


def layer(top, bottom):
    s = {k: top[k] + bottom[k] for k in top if k[1] != "00"}
    d = {k: top[k] - bottom[k] for k in top}
    even, odd = {}, {}
    trace = LAME * (s[0, "10"] + s[1, "01"] + d[2, "00"])
    even[0, "10"] = trace + NORMAL * s[0, "10"]
    even[1, "01"] = trace + NORMAL * s[1, "01"]
    odd[2, "00"] = trace + NORMAL * d[2, "00"]
    even[1, "10"] = even[0, "01"] = SHEAR * (s[1, "10"] + s[0, "01"])
    even[2, "10"] = odd[0, "00"] = SHEAR * (s[2, "10"] + d[0, "00"])
    even[2, "01"] = odd[1, "00"] = SHEAR * (s[2, "01"] + d[1, "00"])
    even[0, "11"] = BEND * s[0, "11"] + d[2, "01"]
    even[1, "11"] = BEND * s[1, "11"] + d[2, "10"]
    twist = s[2, "11"] + d[1, "10"] + d[0, "01"]
    even[2, "11"] = TWIST * (twist + s[2, "11"])
    odd[1, "10"] = TWIST * (twist + d[1, "10"])
    odd[0, "01"] = TWIST * (twist + d[0, "01"])
    odd[0, "10"] = BEND * d[0, "10"] + d[1, "01"]
    odd[1, "01"] = BEND * d[1, "01"] + d[0, "10"]
    odd[2, "10"] = BEND * d[2, "10"] + s[1, "11"]
    odd[2, "01"] = BEND * d[2, "01"] + s[0, "11"]
    for c in range(3):
        odd[c, "11"] = LAST * d[c, "11"]
    return even, odd


PARITIES = ("00", "10", "01", "11")


def stiffness_kernel(
    own, below, above, classes, classes_up, levels, out, low, high,
    runs, x_fields, turned, forces, sums,
):
    low[...] = UNIT * modulus_of(densities(classes[...], levels))
    is_top = lax.axis_index(MESH) == lax.axis_size(MESH) - 1
    high[...] = modulus_of(densities(classes_up[...], levels)) * jnp.where(is_top, 0.0, UNIT)
    lane = lane_index(8)
    inside = ((lane != 0) & (lane != 96), lane != 64, lane != 32)
    before_end = (lane != 95, lane != 63, (lane != 31) & (lane != 127))
    planes = (own, below, above)

    def fetch(h, k):
        for p in range(3):
            for c in range(3):
                u = planes[p][pl.ds(c * 72 + 6 * h + k, 8, stride=216), :]
                runs[(p * 3 + c) * 6 + k] = u
                runs[54 + (p * 3 + c) * 6 + k] = pltpu.roll(u, 1, 1)

    def along_x(k):
        for s in range(9):
            u, rolled = runs[s * 6 + k], runs[54 + s * 6 + k]
            back = jnp.where(inside[k % 3], rolled, 0.0)
            if k % 3:
                back = jnp.where(lane == 0, runs[54 + s * 6 + k - 1], back)
            for n, v in enumerate((u + back, u - back)):
                x_fields[n * 63 + s * 7 + k + 1] = v
                turned[n * 63 + s * 7 + k + 1] = pltpu.roll(v, 96, 1)

    def element_forces(h, k):
        own_f, below_f, above_f = {}, {}, {}
        for p, group in enumerate((own_f, below_f, above_f)):
            for c in range(3):
                for n, name in enumerate("01"):
                    at = n * 63 + (p * 3 + c) * 7 + k
                    row = jnp.where(lane < 96, turned[at], turned[at + 1])
                    here = x_fields[at + 1]
                    group[c, name + "0"] = here + row
                    group[c, name + "1"] = here - row
        even, odd = layer(own_f, below_f)
        even_up, odd_up = layer(above_f, own_f)
        weight = jnp.broadcast_to(low[pl.ds(6 * h + k, 1), :], (8, LANES))
        weight_up = jnp.broadcast_to(high[pl.ds(6 * h + k, 1), :], (8, LANES))
        for c in range(3):
            f = {"00": weight * odd[c, "00"] - weight_up * odd_up[c, "00"]}
            for n in PARITIES[1:]:
                f[n] = weight * (even[c, n] + odd[c, n]) + weight_up * (
                    even_up[c, n] - odd_up[c, n]
                )
            base = k * 12 + c * 4
            forces[base] = f["00"] + f["10"]
            forces[base + 1] = f["01"] + f["11"]
            forces[base + 2] = pltpu.roll(f["00"] - f["10"], 127, 1)
            forces[base + 3] = pltpu.roll(f["01"] - f["11"], 127, 1)
        if k == 5:
            for at in range(0, 126, 7):
                turned[at] = turned[at + 6]

    def gather_x(k):
        for c in range(3):
            pair = []
            for y in range(2):
                base = k * 12 + c * 4 + y
                from_right = jnp.where(before_end[k % 3], forces[base + 2], 0.0)
                if k % 3 < 2:
                    from_right = jnp.where(lane == 127, forces[base + 14], from_right)
                pair.append(forces[base] + from_right)
            sums[c * 7 + k + 1] = pair[0] + pair[1]
            sums[21 + c * 7 + k + 1] = pltpu.roll(pair[0] - pair[1], 32, 1)

    def gather_y(h, k):
        run = jnp.maximum(6 * h + k - 1, 0)
        row = lax.div(run, 9) * 216 + lax.rem(run, 9)
        for c in range(3):
            at = c * 7 + k
            turned_back = jnp.where(lane < 32, sums[21 + at], sums[22 + at])
            out[pl.ds(row + c * 9, 8, stride=27), :] = sums[at] + turned_back
        if k == 5:
            for at in range(0, 42, 7):
                sums[at] = sums[at + 6]

    zero = jnp.zeros((8, LANES), jnp.float32)
    for at in range(0, 126, 7):
        turned[at] = zero
    for at in range(0, 42, 7):
        sums[at] = zero

    def step(t, carry=None):
        fixed = isinstance(t, int)
        stages = (
            (0, 4, 16, lambda k: gather_y(t - 4, k)),
            (1, 3, 15, gather_x),
            (1, 2, 14, lambda k: element_forces(t - 2, k)),
            (2, 1, 13, along_x),
            (3, 0, 12, lambda k: fetch(t, k)),
        )
        for turn in range(9):
            for delay, start, end, stage in stages:
                if 0 <= turn - delay < 6 and (not fixed or start <= t < end):
                    stage(turn - delay)
        return carry

    for t in range(4):
        step(t)
    lax.fori_loop(4, 12, step, 0)
    for t in range(12, 16):
        step(t)
    for c in range(3):
        out[pl.ds(7 * 216 + 8 + c * 9, 8, stride=27), :] = sums[c * 7] + jnp.where(
            lane < 32, sums[21 + c * 7], 0.0
        )


def mass_kernel(basis, classes, levels, mass, band_density, density):
    density[...] = densities(classes[...], levels)
    band = lax.axis_index(MODES)
    acc = jnp.zeros((64, 64), jnp.float32)
    for q in range(9):
        row = density[pl.ds(band * 9 + q, 1), :]
        band_density[pl.ds(q, 1), :] = row
        for c in range(3):
            b = basis[pl.ds(c * 9 + q, 64, stride=27), :]
            acc = acc + dot(b, b * row, ((1,), (1,)))
    mass[...] = acc


def square_index():
    row = lax.broadcasted_iota(jnp.int32, (64, 64), 0)
    return row, lax.broadcasted_iota(jnp.int32, (64, 64), 1)


def gram_kernel(basis, image, mass, out):
    acc = jnp.zeros((64, 64), jnp.float32)
    for t in range(27):
        b = basis[pl.ds(t, 64, stride=27), :]
        v = image[pl.ds(t, 64, stride=27), :]
        acc = acc + dot(b, v, ((1,), (1,)))
    row, column = square_index()
    mass = mass[...]
    packed = jnp.where(row >= column, acc, mass)
    diagonal = jnp.sum(jnp.where(row == column, mass, 0.0), 0, keepdims=True)
    top = jnp.concatenate([packed[:32], packed[32:]], 1)
    last = jnp.broadcast_to(jnp.concatenate([diagonal, diagonal], 1), (8, LANES))
    block = jnp.concatenate([top, last], 0)
    for k in range(16):
        out[k] = block


def unpacked(block):
    row, column = square_index()
    packed = jnp.concatenate([block[:32, :64], block[:32, 64:]], 0)
    other = jnp.transpose(packed)
    diagonal = jnp.broadcast_to(block[32:33, :64], (64, 64))
    stiff = jnp.where(row >= column, packed, other)
    mass = jnp.where(row == column, diagonal, jnp.where(row < column, packed, other))
    return stiff, mass


def dot(a, b, dims):
    return lax.dot_general(
        a, b, (dims, ((), ())), precision=highest, preferred_element_type=jnp.float32
    )


def inverse_factor(mass):
    row = lax.broadcasted_iota(jnp.int32, (64, LANES), 0)
    lane = lax.broadcasted_iota(jnp.int32, (64, LANES), 1)
    start = jnp.where(
        lane < 64,
        jnp.concatenate([mass, mass], 1),
        jnp.where(lane - 64 == row, 1.0, 0.0),
    )
    w = [start[8 * i : 8 * i + 8] for i in range(8)]
    row_in_block = lax.broadcasted_iota(jnp.int32, (8, LANES), 0)

    def spread(pair):
        return [
            {
                i: jnp.broadcast_to(w[i][:, k : k + 1], (8, LANES))
                for i in range(2 * pair // 8, 8)
            }
            for k in (2 * pair, 2 * pair + 1)
        ]

    def at(column, k):
        return column[k // 8][k % 8 : k % 8 + 1]

    waiting = {pair: spread(pair) for pair in range(AHEAD)}
    for pair in range(32):
        if pair + AHEAD < 32:
            waiting[pair + AHEAD] = spread(pair + AHEAD)
        c0, c1 = waiting.pop(pair)
        k = 2 * pair
        a, b, d = at(c0, k), at(c0, k + 1), at(c1, k + 1)
        inv = 1.0 / (a * d - b * b)
        da, db, dd = a * inv, b * inv, d * inv
        for later, columns in waiting.items():
            for n, column in enumerate(columns):
                p0, p1 = at(c0, 2 * later + n), at(c1, 2 * later + n)
                y0, y1 = dd * p0 - db * p1, da * p1 - db * p0
                for i in column:
                    column[i] = column[i] - c0[i] * y0 - c1[i] * y1
        r0, r1 = at(w, k), at(w, k + 1)
        x0, x1 = dd * r0 - db * r1, da * r1 - db * r0
        for i in range((k + 2) // 8, 8):
            new = w[i] - c0[i] * x0 - c1[i] * x1
            w[i] = jnp.where(row_in_block + 8 * i > k + 1, new, w[i]) if 8 * i < k + 2 else new
    w = jnp.concatenate(w, 0)
    diagonal = jnp.sum(jnp.where(lane == row, w, 0.0), 1, keepdims=True)
    left = jnp.sum(jnp.where(lane == row - 1, w, 0.0), 1, keepdims=True)
    odd = row % 2 == 1
    up = pltpu.roll(w, 1, 0)
    up_diagonal = pltpu.roll(jnp.broadcast_to(diagonal, (64, LANES)), 1, 0)
    ratio = jnp.where(odd, left / jnp.where(odd, up_diagonal, 1.0), 0.0)
    pivot = diagonal - ratio * left
    scaled = (w - ratio * up) * lax.rsqrt(pivot)
    return scaled[:, 64:]


def residual_kernel(total_dofs, gram, basis, image, density, out, ritz_ref):
    scale = 1.0 / total_dofs
    stiff, mass = unpacked(gram[...] * scale)
    inverse = inverse_factor(mass)
    ritz = dot(dot(inverse, stiff, ((1,), (0,))), inverse, ((1,), (1,)))
    ritz_ref[...] = ritz
    mixed = dot(ritz, inverse, ((0,), (0,)))
    weights = jnp.concatenate([inverse, -mixed], 1)
    for c in range(3):
        for q in range(9):
            t = c * 9 + q
            b = basis[pl.ds(t, 64, stride=27), :]
            v = image[pl.ds(t, 64, stride=27), :]
            m = b * density[pl.ds(q, 1), :]
            out[pl.ds(t, 64, stride=27), :] = dot(
                weights, jnp.concatenate([v, m], 0), ((1,), (0,))
            )


def join_kernel(x_ref, out_ref):
    def piece(p, carry):
        for c in range(3):
            for q in range(9):
                out_ref[pl.ds(c * 72 + p * 9 + q, 8, stride=216), :] = x_ref[
                    pl.ds(p * 216 + c * 9 + q, 8, stride=27), :
                ]
        return carry

    lax.fori_loop(0, 8, piece, 0)


def room(mib):
    return pltpu.CompilerParams(vmem_limit_bytes=mib << 20)


def f32(*shape):
    return jax.ShapeDtypeStruct(shape, jnp.float32)


def total_sum(x):
    layer_axes = ("mesh_0", "modes_0", "modes_1")
    x = jnp.sum(lax.all_to_all(x, layer_axes, split_axis=0, concat_axis=0, tiled=True), 0)
    x = x + lax.ppermute(x, "mesh_2", [(0, 1), (1, 0)])
    x = jnp.broadcast_to(x[None], (8, *x.shape))
    return jnp.sum(lax.all_to_all(x, "mesh_1", split_axis=0, concat_axis=0, tiled=True), 0)


def per_device(subspace, classes, level_density):
    total_dofs = 3 * NX * NY * subspace.shape[2] * lax.axis_size(MESH)
    flat = subspace.reshape(1728, LANES)
    classes = classes.reshape(72, LANES)
    below = shifted(flat, MESH, 1)
    above = shifted(flat, MESH, -1)
    classes_up = shifted(classes, MESH, -1)
    split = pl.pallas_call(
        split_kernel,
        in_specs=[HBM],
        out_specs=HBM,
        out_shape=f32(1728, LANES),
        scratch_shapes=[
            pltpu.VMEM((3, 8, 72, LANES), jnp.float32),
            pltpu.VMEM((1728, LANES), jnp.float32),
            pltpu.SemaphoreType.DMA((3,)),
            pltpu.SemaphoreType.DMA((8,)),
        ],
        compiler_params=room(4),
        cost_estimate=pl.CostEstimate(flops=10**5, bytes_accessed=1_800_000, transcendentals=0),
        name="split",
    )
    pieces = split(pltpu.with_memory_space_constraint(flat.reshape(8, 3, 72, LANES), pltpu.HBM))

    def all_to_all(x):
        x = x.reshape(8, 216, LANES)
        return lax.all_to_all(x, MODES, split_axis=0, concat_axis=0, tiled=True).reshape(1728, LANES)

    basis = all_to_all(pieces)
    image_pieces = pl.pallas_call(
        stiffness_kernel,
        in_specs=[VMEM] * 5 + [SMEM],
        out_specs=VMEM,
        out_shape=f32(1728, LANES),
        scratch_shapes=[pltpu.VMEM((72, LANES), jnp.float32)] * 2
        + [pltpu.VMEM((n, 8, LANES), jnp.float32) for n in (108, 126, 126, 72, 42)],
        compiler_params=room(12),
        cost_estimate=pl.CostEstimate(
            flops=27_000_000, bytes_accessed=3_600_000, transcendentals=0
        ),
        name="stiffness",
    )(flat, below, above, classes, classes_up, level_density)
    image = all_to_all(image_pieces)
    mass, band_density = pl.pallas_call(
        mass_kernel,
        in_specs=[VMEM, VMEM, SMEM],
        out_specs=[VMEM, VMEM],
        out_shape=[f32(64, 64), f32(16, LANES)],
        scratch_shapes=[pltpu.VMEM((72, LANES), jnp.float32)],
        compiler_params=room(8),
        cost_estimate=pl.CostEstimate(flops=10**8, bytes_accessed=900_000, transcendentals=0),
        name="mass",
    )(basis, classes, level_density)
    local = pl.pallas_call(
        gram_kernel,
        in_specs=[VMEM] * 3,
        out_specs=VMEM,
        out_shape=f32(16, 40, LANES),
        compiler_params=room(8),
        name="grams",
    )(basis, image, mass)
    gram = total_sum(local)
    residual_pieces, ritz_matrix = pl.pallas_call(
        functools.partial(residual_kernel, total_dofs),
        in_specs=[VMEM] * 4,
        out_specs=[VMEM, VMEM],
        out_shape=[f32(1728, LANES), f32(64, 64)],
        compiler_params=room(12),
        name="residual",
    )(gram, basis, image, band_density)
    joined = pl.pallas_call(
        join_kernel,
        in_specs=[VMEM],
        out_specs=VMEM,
        out_shape=f32(1728, LANES),
        compiler_params=room(8),
        name="join",
    )(all_to_all(residual_pieces))
    return (joined.reshape(subspace.shape), ritz_matrix)


def solution(mesh):
    split = Mesh(
        mesh.devices.reshape(2, 8, 2, 2, 4), ("mesh_0", "mesh_1", "mesh_2", "modes_0", "modes_1")
    )
    placed = (P(MODES, None, MESH, None), P(MESH, None), P())
    return jax.shard_map(
        per_device,
        mesh=split,
        in_specs=placed,
        out_specs=(P(MODES, None, MESH, None), P()),
        check_vma=False,
    )
```

```python
import functools

import jax
import jax.numpy as jnp
import numpy as np
from jax import lax
from jax.experimental import pallas as pl
from jax.experimental.pallas import tpu as pltpu
from jax.sharding import Mesh
from jax.sharding import PartitionSpec as P


NX = 96
NY = 96
LANES = 128
MODES = ("modes_0", "modes_1")
MESH = ("mesh_0", "mesh_1", "mesh_2")

highest = lax.Precision.HIGHEST
floor_modulus = 0.001
AHEAD = 2
VMEM = pl.BlockSpec(memory_space=pltpu.VMEM)
SMEM = pl.BlockSpec(memory_space=pltpu.SMEM)
HBM = pl.BlockSpec(memory_space=pltpu.HBM)


def shifted(x, axis, by):
    size = lax.axis_size(axis)
    pairs = [(i, i + by) for i in range(size) if 0 <= i + by < size]
    return lax.ppermute(x, axis, pairs)


def element_matrix():
    poisson_ratio = 0.3
    lame_first = poisson_ratio / ((1 + poisson_ratio) * (1 - 2 * poisson_ratio))
    shear_modulus = 1.0 / (2 * (1 + poisson_ratio))
    elastic = np.zeros((6, 6))
    elastic[:3, :3] = lame_first
    for normal_index in range(3):
        elastic[normal_index, normal_index] = lame_first + 2 * shear_modulus
        elastic[normal_index + 3, normal_index + 3] = shear_modulus
    corner_signs = [
        (1 - 2 * (corner & 1), 1 - 2 * (corner >> 1 & 1), 1 - 2 * (corner >> 2))
        for corner in range(8)
    ]
    gauss_point = 1.0 / np.sqrt(3.0)
    matrix = np.zeros((24, 24))
    for gauss_x in (-gauss_point, gauss_point):
        for gauss_y in (-gauss_point, gauss_point):
            for gauss_z in (-gauss_point, gauss_point):
                strain = np.zeros((6, 24))
                for corner in range(8):
                    sign_x, sign_y, sign_z = corner_signs[corner]
                    deriv_x = 2 * sign_x * (1 + sign_y * gauss_y) * (1 + sign_z * gauss_z) / 8
                    deriv_y = 2 * sign_y * (1 + sign_x * gauss_x) * (1 + sign_z * gauss_z) / 8
                    deriv_z = 2 * sign_z * (1 + sign_x * gauss_x) * (1 + sign_y * gauss_y) / 8
                    column = 3 * corner
                    strain[0, column] = deriv_x
                    strain[1, column + 1] = deriv_y
                    strain[2, column + 2] = deriv_z
                    strain[3, column] = deriv_y
                    strain[3, column + 1] = deriv_x
                    strain[4, column + 1] = deriv_z
                    strain[4, column + 2] = deriv_y
                    strain[5, column] = deriv_z
                    strain[5, column + 2] = deriv_x
                matrix = matrix + strain.T @ elastic @ strain / 8
    return matrix.reshape(8, 3, 8, 3)


def parity_coefficients():
    signs = np.array([[(-1.0) ** bin(p & n).count("1") for n in range(8)] for p in range(8)])
    block = np.einsum("qn,ncmd,pm->qcpd", signs, element_matrix(), signs) / 64
    unit = block[3, 0, 6, 2]
    ratios = tuple(
        float(np.float32(v / unit))
        for v in (
            block[1, 0, 2, 1],
            block[1, 0, 1, 0] - block[1, 0, 2, 1],
            block[1, 1, 1, 1],
            block[3, 0, 3, 0],
            block[3, 2, 5, 1],
            block[7, 0, 7, 0],
        )
    )
    return (float(np.float32(unit)), *ratios)


UNIT, LAME, NORMAL, SHEAR, BEND, TWIST, LAST = parity_coefficients()


def lane_index(rows):
    return lax.broadcasted_iota(jnp.int32, (rows, LANES), 1)


def modulus_of(density):
    return floor_modulus + (1.0 - floor_modulus) * density * density * density


def densities(classes, levels):
    density = jnp.zeros(classes.shape, jnp.float32)
    for level in range(16):
        density = jnp.where(classes == level, levels[level], density)
    return density


def split_kernel(x_hbm, pieces_hbm, x_ref, pieces_ref, load, store):
    loads = [
        pltpu.make_async_copy(x_hbm.at[:, c], x_ref.at[c], load.at[c]) for c in range(3)
    ]
    for copy in loads:
        copy.start()
    stores = []
    for c in range(3):
        loads[c].wait()
        for p in range(8):
            for q in range(9):
                pieces_ref[pl.ds(p * 216 + c * 9 + q, 8, stride=27), :] = x_ref[
                    c, :, p * 9 + q, :
                ]
            if c == 2:
                part = pl.ds(p * 216, 216)
                stores.append(
                    pltpu.make_async_copy(pieces_ref.at[part], pieces_hbm.at[part], store.at[p])
                )
                stores[-1].start()
    for copy in stores:
        copy.wait()


def layer(top, bottom):
    s = {k: top[k] + bottom[k] for k in top if k[1] != "00"}
    d = {k: top[k] - bottom[k] for k in top}
    even, odd = {}, {}
    trace = LAME * (s[0, "10"] + s[1, "01"] + d[2, "00"])
    even[0, "10"] = trace + NORMAL * s[0, "10"]
    even[1, "01"] = trace + NORMAL * s[1, "01"]
    odd[2, "00"] = trace + NORMAL * d[2, "00"]
    even[1, "10"] = even[0, "01"] = SHEAR * (s[1, "10"] + s[0, "01"])
    even[2, "10"] = odd[0, "00"] = SHEAR * (s[2, "10"] + d[0, "00"])
    even[2, "01"] = odd[1, "00"] = SHEAR * (s[2, "01"] + d[1, "00"])
    even[0, "11"] = BEND * s[0, "11"] + d[2, "01"]
    even[1, "11"] = BEND * s[1, "11"] + d[2, "10"]
    twist = s[2, "11"] + d[1, "10"] + d[0, "01"]
    even[2, "11"] = TWIST * (twist + s[2, "11"])
    odd[1, "10"] = TWIST * (twist + d[1, "10"])
    odd[0, "01"] = TWIST * (twist + d[0, "01"])
    odd[0, "10"] = BEND * d[0, "10"] + d[1, "01"]
    odd[1, "01"] = BEND * d[1, "01"] + d[0, "10"]
    odd[2, "10"] = BEND * d[2, "10"] + s[1, "11"]
    odd[2, "01"] = BEND * d[2, "01"] + s[0, "11"]
    for c in range(3):
        odd[c, "11"] = LAST * d[c, "11"]
    return even, odd


PARITIES = ("00", "10", "01", "11")


def stiffness_kernel(
    own, below, above, classes, classes_up, levels, out, low, high,
    runs, x_fields, turned, forces, sums,
):
    low[...] = UNIT * modulus_of(densities(classes[...], levels))
    is_top = lax.axis_index(MESH) == lax.axis_size(MESH) - 1
    high[...] = modulus_of(densities(classes_up[...], levels)) * jnp.where(is_top, 0.0, UNIT)
    lane = lane_index(8)
    inside = ((lane != 0) & (lane != 96), lane != 64, lane != 32)
    before_end = (lane != 95, lane != 63, (lane != 31) & (lane != 127))
    planes = (own, below, above)

    def fetch(h, k):
        for p in range(3):
            for c in range(3):
                u = planes[p][pl.ds(c * 72 + 6 * h + k, 8, stride=216), :]
                runs[(p * 3 + c) * 6 + k] = u
                runs[54 + (p * 3 + c) * 6 + k] = pltpu.roll(u, 1, 1)

    def along_x(k):
        for s in range(9):
            u, rolled = runs[s * 6 + k], runs[54 + s * 6 + k]
            back = jnp.where(inside[k % 3], rolled, 0.0)
            if k % 3:
                back = jnp.where(lane == 0, runs[54 + s * 6 + k - 1], back)
            for n, v in enumerate((u + back, u - back)):
                x_fields[n * 63 + s * 7 + k + 1] = v
                turned[n * 63 + s * 7 + k + 1] = pltpu.roll(v, 96, 1)

    def element_forces(h, k):
        own_f, below_f, above_f = {}, {}, {}
        for p, group in enumerate((own_f, below_f, above_f)):
            for c in range(3):
                for n, name in enumerate("01"):
                    at = n * 63 + (p * 3 + c) * 7 + k
                    row = jnp.where(lane < 96, turned[at], turned[at + 1])
                    here = x_fields[at + 1]
                    group[c, name + "0"] = here + row
                    group[c, name + "1"] = here - row
        even, odd = layer(own_f, below_f)
        even_up, odd_up = layer(above_f, own_f)
        weight = jnp.broadcast_to(low[pl.ds(6 * h + k, 1), :], (8, LANES))
        weight_up = jnp.broadcast_to(high[pl.ds(6 * h + k, 1), :], (8, LANES))
        for c in range(3):
            f = {"00": weight * odd[c, "00"] - weight_up * odd_up[c, "00"]}
            for n in PARITIES[1:]:
                f[n] = weight * (even[c, n] + odd[c, n]) + weight_up * (
                    even_up[c, n] - odd_up[c, n]
                )
            base = k * 12 + c * 4
            forces[base] = f["00"] + f["10"]
            forces[base + 1] = f["01"] + f["11"]
            forces[base + 2] = pltpu.roll(f["00"] - f["10"], 127, 1)
            forces[base + 3] = pltpu.roll(f["01"] - f["11"], 127, 1)
        if k == 5:
            for at in range(0, 126, 7):
                turned[at] = turned[at + 6]

    def gather_x(k):
        for c in range(3):
            pair = []
            for y in range(2):
                base = k * 12 + c * 4 + y
                from_right = jnp.where(before_end[k % 3], forces[base + 2], 0.0)
                if k % 3 < 2:
                    from_right = jnp.where(lane == 127, forces[base + 14], from_right)
                pair.append(forces[base] + from_right)
            sums[c * 7 + k + 1] = pair[0] + pair[1]
            sums[21 + c * 7 + k + 1] = pltpu.roll(pair[0] - pair[1], 32, 1)

    def gather_y(h, k):
        run = jnp.maximum(6 * h + k - 1, 0)
        row = lax.div(run, 9) * 216 + lax.rem(run, 9)
        for c in range(3):
            at = c * 7 + k
            turned_back = jnp.where(lane < 32, sums[21 + at], sums[22 + at])
            out[pl.ds(row + c * 9, 8, stride=27), :] = sums[at] + turned_back
        if k == 5:
            for at in range(0, 42, 7):
                sums[at] = sums[at + 6]

    zero = jnp.zeros((8, LANES), jnp.float32)
    for at in range(0, 126, 7):
        turned[at] = zero
    for at in range(0, 42, 7):
        sums[at] = zero

    def step(t, carry=None):
        fixed = isinstance(t, int)
        stages = (
            (0, 4, 16, lambda k: gather_y(t - 4, k)),
            (1, 3, 15, gather_x),
            (1, 2, 14, lambda k: element_forces(t - 2, k)),
            (2, 1, 13, along_x),
            (3, 0, 12, lambda k: fetch(t, k)),
        )
        for turn in range(9):
            for delay, start, end, stage in stages:
                if 0 <= turn - delay < 6 and (not fixed or start <= t < end):
                    stage(turn - delay)
        return carry

    for t in range(4):
        step(t)
    lax.fori_loop(4, 12, step, 0)
    for t in range(12, 16):
        step(t)
    for c in range(3):
        out[pl.ds(7 * 216 + 8 + c * 9, 8, stride=27), :] = sums[c * 7] + jnp.where(
            lane < 32, sums[21 + c * 7], 0.0
        )


def halves(x):
    high = x.astype(jnp.bfloat16)
    return high, (x - high.astype(jnp.float32)).astype(jnp.bfloat16)


def band_densities(classes, levels, density):
    density[...] = densities(classes[...], levels)
    band = lax.axis_index(MODES)
    return [density[pl.ds(band * 9 + q, 1), :] for q in range(9)]


def square_index():
    row = lax.broadcasted_iota(jnp.int32, (64, 64), 0)
    return row, lax.broadcasted_iota(jnp.int32, (64, 64), 1)


def gram_kernel(basis, image, classes, levels, out, density):
    rows = band_densities(classes, levels, density)
    acc = jnp.zeros((64, LANES), jnp.float32)
    for c in range(3):
        left, right = [], []
        for q in range(9):
            b = basis[pl.ds(c * 9 + q, 64, stride=27), :]
            v = image[pl.ds(c * 9 + q, 64, stride=27), :]
            b_high, b_low = halves(b)
            v_high, v_low = halves(jnp.concatenate([v, b * rows[q]], 0))
            left += [b_high, b_low, b_high]
            right += [v_high, v_high, v_low]
        acc = acc + lax.dot_general(
            jnp.concatenate(left, 1),
            jnp.concatenate(right, 1),
            (((1,), (1,)), ((), ())),
            preferred_element_type=jnp.float32,
        )
    acc, mass = acc[:, :64], acc[:, 64:]
    row, column = square_index()
    packed = jnp.where(row >= column, acc, mass)
    diagonal = jnp.sum(jnp.where(row == column, mass, 0.0), 0, keepdims=True)
    top = jnp.concatenate([packed[:32], packed[32:]], 1)
    last = jnp.broadcast_to(jnp.concatenate([diagonal, diagonal], 1), (8, LANES))
    block = jnp.concatenate([top, last], 0)
    for k in range(16):
        out[k] = block


def unpacked(block):
    row, column = square_index()
    packed = jnp.concatenate([block[:32, :64], block[:32, 64:]], 0)
    other = jnp.transpose(packed)
    diagonal = jnp.broadcast_to(block[32:33, :64], (64, 64))
    stiff = jnp.where(row >= column, packed, other)
    mass = jnp.where(row == column, diagonal, jnp.where(row < column, packed, other))
    return stiff, mass


def dot(a, b, dims):
    return lax.dot_general(
        a, b, (dims, ((), ())), precision=highest, preferred_element_type=jnp.float32
    )


def inverse_factor(mass):
    row = lax.broadcasted_iota(jnp.int32, (64, LANES), 0)
    lane = lax.broadcasted_iota(jnp.int32, (64, LANES), 1)
    start = jnp.where(
        lane < 64,
        jnp.concatenate([mass, mass], 1),
        jnp.where(lane - 64 == row, 1.0, 0.0),
    )
    w = [start[8 * i : 8 * i + 8] for i in range(8)]
    row_in_block = lax.broadcasted_iota(jnp.int32, (8, LANES), 0)

    def spread(pair):
        return [
            {
                i: jnp.broadcast_to(w[i][:, k : k + 1], (8, LANES))
                for i in range(2 * pair // 8, 8)
            }
            for k in (2 * pair, 2 * pair + 1)
        ]

    def at(column, k):
        return column[k // 8][k % 8 : k % 8 + 1]

    waiting = {pair: spread(pair) for pair in range(AHEAD)}
    for pair in range(32):
        if pair + AHEAD < 32:
            waiting[pair + AHEAD] = spread(pair + AHEAD)
        c0, c1 = waiting.pop(pair)
        k = 2 * pair
        a, b, d = at(c0, k), at(c0, k + 1), at(c1, k + 1)
        inv = 1.0 / (a * d - b * b)
        da, db, dd = a * inv, b * inv, d * inv
        for later, columns in waiting.items():
            for n, column in enumerate(columns):
                p0, p1 = at(c0, 2 * later + n), at(c1, 2 * later + n)
                y0, y1 = dd * p0 - db * p1, da * p1 - db * p0
                for i in column:
                    column[i] = column[i] - c0[i] * y0 - c1[i] * y1
        r0, r1 = at(w, k), at(w, k + 1)
        x0, x1 = dd * r0 - db * r1, da * r1 - db * r0
        for i in range((k + 2) // 8, 8):
            new = w[i] - c0[i] * x0 - c1[i] * x1
            w[i] = jnp.where(row_in_block + 8 * i > k + 1, new, w[i]) if 8 * i < k + 2 else new
    w = jnp.concatenate(w, 0)
    diagonal = jnp.sum(jnp.where(lane == row, w, 0.0), 1, keepdims=True)
    left = jnp.sum(jnp.where(lane == row - 1, w, 0.0), 1, keepdims=True)
    odd = row % 2 == 1
    up = pltpu.roll(w, 1, 0)
    up_diagonal = pltpu.roll(jnp.broadcast_to(diagonal, (64, LANES)), 1, 0)
    ratio = jnp.where(odd, left / jnp.where(odd, up_diagonal, 1.0), 0.0)
    pivot = diagonal - ratio * left
    scaled = (w - ratio * up) * lax.rsqrt(pivot)
    return scaled[:, 64:]


def residual_kernel(total_dofs, gram, basis, image, classes, levels, out, ritz_ref, density):
    rows = band_densities(classes, levels, density)
    stiff, mass = unpacked(gram[...] * (1.0 / total_dofs))
    inverse = inverse_factor(mass)
    ritz = dot(dot(inverse, stiff, ((1,), (0,))), inverse, ((1,), (1,)))
    ritz_ref[...] = ritz
    mixed = dot(ritz, inverse, ((0,), (0,)))
    high, low = halves(jnp.concatenate([inverse, -mixed], 1))
    weights = jnp.concatenate([high, low, high], 1)
    for q in range(9):
        for c in range(3):
            t = c * 9 + q
            b = basis[pl.ds(t, 64, stride=27), :]
            v = image[pl.ds(t, 64, stride=27), :]
            x_high, x_low = halves(jnp.concatenate([v, b * rows[q]], 0))
            out[pl.ds(t, 64, stride=27), :] = lax.dot_general(
                weights,
                jnp.concatenate([x_high, x_high, x_low], 0),
                (((1,), (0,)), ((), ())),
                preferred_element_type=jnp.float32,
            )


def join_kernel(x_ref, out_ref):
    def piece(p, carry):
        for c in range(3):
            for q in range(9):
                out_ref[pl.ds(c * 72 + p * 9 + q, 8, stride=216), :] = x_ref[
                    pl.ds(p * 216 + c * 9 + q, 8, stride=27), :
                ]
        return carry

    lax.fori_loop(0, 8, piece, 0)


def room(mib):
    return pltpu.CompilerParams(vmem_limit_bytes=mib << 20)


def f32(*shape):
    return jax.ShapeDtypeStruct(shape, jnp.float32)


def total_sum(x):
    layer_axes = ("mesh_0", "modes_0", "modes_1")
    x = jnp.sum(lax.all_to_all(x, layer_axes, split_axis=0, concat_axis=0, tiled=True), 0)
    x = x + lax.ppermute(x, "mesh_2", [(0, 1), (1, 0)])
    x = jnp.broadcast_to(x[None], (8, *x.shape))
    return jnp.sum(lax.all_to_all(x, "mesh_1", split_axis=0, concat_axis=0, tiled=True), 0)


def per_device(subspace, classes, level_density):
    total_dofs = 3 * NX * NY * subspace.shape[2] * lax.axis_size(MESH)
    flat = subspace.reshape(1728, LANES)
    classes = classes.reshape(72, LANES)
    below = shifted(flat, MESH, 1)
    above = shifted(flat, MESH, -1)
    classes_up = shifted(classes, MESH, -1)
    split = pl.pallas_call(
        split_kernel,
        in_specs=[HBM],
        out_specs=HBM,
        out_shape=f32(1728, LANES),
        scratch_shapes=[
            pltpu.VMEM((3, 8, 72, LANES), jnp.float32),
            pltpu.VMEM((1728, LANES), jnp.float32),
            pltpu.SemaphoreType.DMA((3,)),
            pltpu.SemaphoreType.DMA((8,)),
        ],
        compiler_params=room(4),
        cost_estimate=pl.CostEstimate(flops=10**5, bytes_accessed=1_800_000, transcendentals=0),
        name="split",
    )
    pieces = split(pltpu.with_memory_space_constraint(flat.reshape(8, 3, 72, LANES), pltpu.HBM))

    def all_to_all(x):
        x = x.reshape(8, 216, LANES)
        return lax.all_to_all(x, MODES, split_axis=0, concat_axis=0, tiled=True).reshape(1728, LANES)

    basis = all_to_all(pieces)
    image_pieces = pl.pallas_call(
        stiffness_kernel,
        in_specs=[VMEM] * 5 + [SMEM],
        out_specs=VMEM,
        out_shape=f32(1728, LANES),
        scratch_shapes=[pltpu.VMEM((72, LANES), jnp.float32)] * 2
        + [pltpu.VMEM((n, 8, LANES), jnp.float32) for n in (108, 126, 126, 72, 42)],
        compiler_params=room(12),
        cost_estimate=pl.CostEstimate(
            flops=27_000_000, bytes_accessed=3_600_000, transcendentals=0
        ),
        name="stiffness",
    )(
        pltpu.with_memory_space_constraint(flat, pltpu.HBM),
        below,
        above,
        pltpu.with_memory_space_constraint(classes, pltpu.HBM),
        classes_up,
        level_density,
    )
    image = all_to_all(image_pieces)
    local = pl.pallas_call(
        gram_kernel,
        in_specs=[VMEM] * 3 + [SMEM],
        out_specs=VMEM,
        out_shape=f32(16, 40, LANES),
        scratch_shapes=[pltpu.VMEM((72, LANES), jnp.float32)],
        compiler_params=room(12),
        name="grams",
    )(basis, image, classes, level_density)
    gram = total_sum(local)
    residual_pieces, ritz_matrix = pl.pallas_call(
        functools.partial(residual_kernel, total_dofs),
        in_specs=[VMEM] * 4 + [SMEM],
        out_specs=[VMEM, VMEM],
        out_shape=[f32(1728, LANES), f32(64, 64)],
        scratch_shapes=[pltpu.VMEM((72, LANES), jnp.float32)],
        compiler_params=room(12),
        name="residual",
    )(gram, basis, image, classes, level_density)
    joined = pl.pallas_call(
        join_kernel,
        in_specs=[VMEM],
        out_specs=VMEM,
        out_shape=f32(1728, LANES),
        compiler_params=room(8),
        name="join",
    )(all_to_all(residual_pieces))
    return (joined.reshape(subspace.shape), ritz_matrix)


def solution(mesh):
    split = Mesh(
        mesh.devices.reshape(2, 8, 2, 2, 4), ("mesh_0", "mesh_1", "mesh_2", "modes_0", "modes_1")
    )
    placed = (P(MODES, None, MESH, None), P(MESH, None), P())
    return jax.shard_map(
        per_device,
        mesh=split,
        in_specs=placed,
        out_specs=(P(MODES, None, MESH, None), P()),
        check_vma=False,
    )
```

```python
import functools

import jax
import jax.numpy as jnp
import numpy as np
from jax import lax
from jax.experimental import pallas as pl
from jax.experimental.pallas import tpu as pltpu
from jax.sharding import Mesh
from jax.sharding import PartitionSpec as P


NX = 96
NY = 96
LANES = 128
MODES = ("modes_0", "modes_1")
MESH = ("mesh_0", "mesh_1", "mesh_2")

highest = lax.Precision.HIGHEST
floor_modulus = 0.001
AHEAD = 2
VMEM = pl.BlockSpec(memory_space=pltpu.VMEM)
SMEM = pl.BlockSpec(memory_space=pltpu.SMEM)
HBM = pl.BlockSpec(memory_space=pltpu.HBM)


def shifted(x, axis, by):
    size = lax.axis_size(axis)
    pairs = [(i, i + by) for i in range(size) if 0 <= i + by < size]
    return lax.ppermute(x, axis, pairs)


def element_matrix():
    poisson_ratio = 0.3
    lame_first = poisson_ratio / ((1 + poisson_ratio) * (1 - 2 * poisson_ratio))
    shear_modulus = 1.0 / (2 * (1 + poisson_ratio))
    elastic = np.zeros((6, 6))
    elastic[:3, :3] = lame_first
    for normal_index in range(3):
        elastic[normal_index, normal_index] = lame_first + 2 * shear_modulus
        elastic[normal_index + 3, normal_index + 3] = shear_modulus
    corner_signs = [
        (1 - 2 * (corner & 1), 1 - 2 * (corner >> 1 & 1), 1 - 2 * (corner >> 2))
        for corner in range(8)
    ]
    gauss_point = 1.0 / np.sqrt(3.0)
    matrix = np.zeros((24, 24))
    for gauss_x in (-gauss_point, gauss_point):
        for gauss_y in (-gauss_point, gauss_point):
            for gauss_z in (-gauss_point, gauss_point):
                strain = np.zeros((6, 24))
                for corner in range(8):
                    sign_x, sign_y, sign_z = corner_signs[corner]
                    deriv_x = 2 * sign_x * (1 + sign_y * gauss_y) * (1 + sign_z * gauss_z) / 8
                    deriv_y = 2 * sign_y * (1 + sign_x * gauss_x) * (1 + sign_z * gauss_z) / 8
                    deriv_z = 2 * sign_z * (1 + sign_x * gauss_x) * (1 + sign_y * gauss_y) / 8
                    column = 3 * corner
                    strain[0, column] = deriv_x
                    strain[1, column + 1] = deriv_y
                    strain[2, column + 2] = deriv_z
                    strain[3, column] = deriv_y
                    strain[3, column + 1] = deriv_x
                    strain[4, column + 1] = deriv_z
                    strain[4, column + 2] = deriv_y
                    strain[5, column] = deriv_z
                    strain[5, column + 2] = deriv_x
                matrix = matrix + strain.T @ elastic @ strain / 8
    return matrix.reshape(8, 3, 8, 3)


def parity_coefficients():
    signs = np.array([[(-1.0) ** bin(p & n).count("1") for n in range(8)] for p in range(8)])
    block = np.einsum("qn,ncmd,pm->qcpd", signs, element_matrix(), signs) / 64
    unit = block[3, 0, 6, 2]
    ratios = tuple(
        float(np.float32(v / unit))
        for v in (
            block[1, 0, 2, 1],
            block[1, 0, 1, 0] - block[1, 0, 2, 1],
            block[1, 1, 1, 1],
            block[3, 0, 3, 0],
            block[3, 2, 5, 1],
            block[7, 0, 7, 0],
        )
    )
    return (float(np.float32(unit)), *ratios)


UNIT, LAME, NORMAL, SHEAR, BEND, TWIST, LAST = parity_coefficients()


def lane_index(rows):
    return lax.broadcasted_iota(jnp.int32, (rows, LANES), 1)


def modulus_of(density):
    return floor_modulus + (1.0 - floor_modulus) * density * density * density


def densities(classes, levels):
    density = jnp.zeros(classes.shape, jnp.float32)
    for level in range(16):
        density = jnp.where(classes == level, levels[level], density)
    return density


def split_kernel(x_hbm, pieces_hbm, x_ref, pieces_ref, load, store):
    loads = [
        pltpu.make_async_copy(x_hbm.at[:, c], x_ref.at[c], load.at[c]) for c in range(3)
    ]
    for copy in loads:
        copy.start()
    stores = []
    for c in range(3):
        loads[c].wait()
        for p in range(8):
            for q in range(9):
                pieces_ref[pl.ds(p * 216 + c * 9 + q, 8, stride=27), :] = x_ref[
                    c, :, p * 9 + q, :
                ]
            if c == 2:
                part = pl.ds(p * 216, 216)
                stores.append(
                    pltpu.make_async_copy(pieces_ref.at[part], pieces_hbm.at[part], store.at[p])
                )
                stores[-1].start()
    for copy in stores:
        copy.wait()


def layer(top, bottom):
    s = {k: top[k] + bottom[k] for k in top if k[1] != "00"}
    d = {k: top[k] - bottom[k] for k in top}
    even, odd = {}, {}
    trace = LAME * (s[0, "10"] + s[1, "01"] + d[2, "00"])
    even[0, "10"] = trace + NORMAL * s[0, "10"]
    even[1, "01"] = trace + NORMAL * s[1, "01"]
    odd[2, "00"] = trace + NORMAL * d[2, "00"]
    even[1, "10"] = even[0, "01"] = SHEAR * (s[1, "10"] + s[0, "01"])
    even[2, "10"] = odd[0, "00"] = SHEAR * (s[2, "10"] + d[0, "00"])
    even[2, "01"] = odd[1, "00"] = SHEAR * (s[2, "01"] + d[1, "00"])
    even[0, "11"] = BEND * s[0, "11"] + d[2, "01"]
    even[1, "11"] = BEND * s[1, "11"] + d[2, "10"]
    twist = s[2, "11"] + d[1, "10"] + d[0, "01"]
    even[2, "11"] = TWIST * (twist + s[2, "11"])
    odd[1, "10"] = TWIST * (twist + d[1, "10"])
    odd[0, "01"] = TWIST * (twist + d[0, "01"])
    odd[0, "10"] = BEND * d[0, "10"] + d[1, "01"]
    odd[1, "01"] = BEND * d[1, "01"] + d[0, "10"]
    odd[2, "10"] = BEND * d[2, "10"] + s[1, "11"]
    odd[2, "01"] = BEND * d[2, "01"] + s[0, "11"]
    for c in range(3):
        odd[c, "11"] = LAST * d[c, "11"]
    return even, odd


PARITIES = ("00", "10", "01", "11")


def stiffness_kernel(
    own, below, above, classes, classes_up, levels, out, low, high,
    runs, x_fields, turned, forces, sums,
):
    low[...] = UNIT * modulus_of(densities(classes[...], levels))
    is_top = lax.axis_index(MESH) == lax.axis_size(MESH) - 1
    high[...] = modulus_of(densities(classes_up[...], levels)) * jnp.where(is_top, 0.0, UNIT)
    lane = lane_index(8)
    inside = ((lane != 0) & (lane != 96), lane != 64, lane != 32)
    before_end = (lane != 95, lane != 63, (lane != 31) & (lane != 127))
    planes = (own, below, above)

    def fetch(h, k, side):
        for s in range(9):
            u = planes[s // 3][pl.ds(s % 3 * 72 + 6 * h + k, 8, stride=216), :]
            runs[side, s * 6 + k] = u
            runs[side, 54 + s * 6 + k] = pltpu.roll(u, 1, 1)

    def along_x(k, side):
        for s in range(9):
            u, rolled = runs[side, s * 6 + k], runs[side, 54 + s * 6 + k]
            back = jnp.where(inside[k % 3], rolled, 0.0)
            if k % 3:
                back = jnp.where(lane == 0, runs[side, 54 + s * 6 + k - 1], back)
            for n, v in enumerate((u + back, u - back)):
                x_fields[side, n * 54 + s * 6 + k] = v
                turned[side, n * 54 + s * 6 + k] = pltpu.roll(v, 96, 1)

    def element_forces(h, k, side):
        own_f, below_f, above_f = {}, {}, {}
        for p, group in enumerate((own_f, below_f, above_f)):
            for c in range(3):
                for n, name in enumerate("01"):
                    at = n * 54 + (p * 3 + c) * 6 + k
                    last = turned[side, at - 1] if k else turned[1 - side, at + 5]
                    row = jnp.where(lane < 96, last, turned[side, at])
                    here = x_fields[side, at]
                    group[c, name + "0"] = here + row
                    group[c, name + "1"] = here - row
        even, odd = layer(own_f, below_f)
        even_up, odd_up = layer(above_f, own_f)
        weight = jnp.broadcast_to(low[pl.ds(6 * h + k, 1), :], (8, LANES))
        weight_up = jnp.broadcast_to(high[pl.ds(6 * h + k, 1), :], (8, LANES))
        for c in range(3):
            f = {"00": weight * odd[c, "00"] - weight_up * odd_up[c, "00"]}
            for n in PARITIES[1:]:
                f[n] = weight * (even[c, n] + odd[c, n]) + weight_up * (
                    even_up[c, n] - odd_up[c, n]
                )
            base = k * 12 + c * 4
            forces[side, base] = f["00"] + f["10"]
            forces[side, base + 1] = f["01"] + f["11"]
            forces[side, base + 2] = pltpu.roll(f["00"] - f["10"], 127, 1)
            forces[side, base + 3] = pltpu.roll(f["01"] - f["11"], 127, 1)

    def gather_x(k, side):
        for c in range(3):
            pair = []
            for y in range(2):
                base = k * 12 + c * 4 + y
                from_right = jnp.where(before_end[k % 3], forces[side, base + 2], 0.0)
                if k % 3 < 2:
                    from_right = jnp.where(lane == 127, forces[side, base + 14], from_right)
                pair.append(forces[side, base] + from_right)
            sums[side, c * 6 + k] = pair[0] + pair[1]
            sums[side, 18 + c * 6 + k] = pltpu.roll(pair[0] - pair[1], 32, 1)

    def gather_y(h, k, side):
        run = jnp.maximum(6 * h + k - 1, 0)
        row = lax.div(run, 9) * 216 + lax.rem(run, 9)
        for c in range(3):
            at = c * 6 + k
            old_side, old = (side, at - 1) if k else (1 - side, at + 5)
            turned_back = jnp.where(lane < 32, sums[old_side, 18 + old], sums[side, 18 + at])
            out[pl.ds(row + c * 9, 8, stride=27), :] = sums[old_side, old] + turned_back

    zero = jnp.zeros((8, LANES), jnp.float32)
    for s in range(18):
        turned[1, s * 6 + 5] = zero
    for s in range(6):
        sums[1, s * 6 + 5] = zero

    def step(t, parity, fixed=True):
        same, other = parity, 1 - parity
        stages = (
            (4, 16, lambda k: gather_y(t - 4, k, same)),
            (3, 15, lambda k: gather_x(k, other)),
            (2, 14, lambda k: element_forces(t - 2, k, same)),
            (1, 13, lambda k: along_x(k, other)),
            (0, 12, lambda k: fetch(t, k, same)),
        )
        for k in range(6):
            for start, end, stage in stages:
                if not fixed or start <= t < end:
                    stage(k)

    def two_steps(i, carry):
        step(2 * i, 0, False)
        step(2 * i + 1, 1, False)
        return carry

    for t in range(4):
        step(t, t % 2)
    lax.fori_loop(2, 6, two_steps, 0)
    for t in range(12, 16):
        step(t, t % 2)
    for c in range(3):
        out[pl.ds(7 * 216 + 8 + c * 9, 8, stride=27), :] = sums[1, c * 6 + 5] + jnp.where(
            lane < 32, sums[1, 18 + c * 6 + 5], 0.0
        )


def halves(x):
    high = x.astype(jnp.bfloat16)
    return high, (x - high.astype(jnp.float32)).astype(jnp.bfloat16)


def band_densities(classes, levels, density):
    density[...] = densities(classes[...], levels)
    band = lax.axis_index(MODES)
    return [density[pl.ds(band * 9 + q, 1), :] for q in range(9)]


def square_index():
    row = lax.broadcasted_iota(jnp.int32, (64, 64), 0)
    return row, lax.broadcasted_iota(jnp.int32, (64, 64), 1)


def gram_kernel(basis, image, classes, levels, out, density):
    rows = band_densities(classes, levels, density)
    acc = jnp.zeros((64, LANES), jnp.float32)
    for c in range(3):
        left, right = [], []
        for q in range(9):
            b = basis[pl.ds(c * 9 + q, 64, stride=27), :]
            v = image[pl.ds(c * 9 + q, 64, stride=27), :]
            b_high, b_low = halves(b)
            v_high, v_low = halves(jnp.concatenate([v, b * rows[q]], 0))
            left += [b_high, b_low, b_high]
            right += [v_high, v_high, v_low]
        acc = acc + lax.dot_general(
            jnp.concatenate(left, 1),
            jnp.concatenate(right, 1),
            (((1,), (1,)), ((), ())),
            preferred_element_type=jnp.float32,
        )
    acc, mass = acc[:, :64], acc[:, 64:]
    row, column = square_index()
    packed = jnp.where(row >= column, acc, mass)
    diagonal = jnp.sum(jnp.where(row == column, mass, 0.0), 0, keepdims=True)
    top = jnp.concatenate([packed[:32], packed[32:]], 1)
    last = jnp.broadcast_to(jnp.concatenate([diagonal, diagonal], 1), (8, LANES))
    block = jnp.concatenate([top, last], 0)
    for k in range(16):
        out[k] = block


def unpacked(block):
    row, column = square_index()
    packed = jnp.concatenate([block[:32, :64], block[:32, 64:]], 0)
    other = jnp.transpose(packed)
    diagonal = jnp.broadcast_to(block[32:33, :64], (64, 64))
    stiff = jnp.where(row >= column, packed, other)
    mass = jnp.where(row == column, diagonal, jnp.where(row < column, packed, other))
    return stiff, mass


def dot(a, b, dims):
    return lax.dot_general(
        a, b, (dims, ((), ())), precision=highest, preferred_element_type=jnp.float32
    )


def inverse_factor(mass):
    row = lax.broadcasted_iota(jnp.int32, (64, LANES), 0)
    lane = lax.broadcasted_iota(jnp.int32, (64, LANES), 1)
    start = jnp.where(
        lane < 64,
        jnp.concatenate([mass, mass], 1),
        jnp.where(lane - 64 == row, 1.0, 0.0),
    )
    w = [start[8 * i : 8 * i + 8] for i in range(8)]
    row_in_block = lax.broadcasted_iota(jnp.int32, (8, LANES), 0)

    def spread(pair):
        return [
            {
                i: jnp.broadcast_to(w[i][:, k : k + 1], (8, LANES))
                for i in range(2 * pair // 8, 8)
            }
            for k in (2 * pair, 2 * pair + 1)
        ]

    def at(column, k):
        return column[k // 8][k % 8 : k % 8 + 1]

    waiting = {pair: spread(pair) for pair in range(AHEAD)}
    for pair in range(32):
        if pair + AHEAD < 32:
            waiting[pair + AHEAD] = spread(pair + AHEAD)
        c0, c1 = waiting.pop(pair)
        k = 2 * pair
        a, b, d = at(c0, k), at(c0, k + 1), at(c1, k + 1)
        inv = 1.0 / (a * d - b * b)
        da, db, dd = a * inv, b * inv, d * inv
        for later, columns in waiting.items():
            for n, column in enumerate(columns):
                p0, p1 = at(c0, 2 * later + n), at(c1, 2 * later + n)
                y0, y1 = dd * p0 - db * p1, da * p1 - db * p0
                for i in column:
                    column[i] = column[i] - c0[i] * y0 - c1[i] * y1
        r0, r1 = at(w, k), at(w, k + 1)
        x0, x1 = dd * r0 - db * r1, da * r1 - db * r0
        for i in range((k + 2) // 8, 8):
            new = w[i] - c0[i] * x0 - c1[i] * x1
            w[i] = jnp.where(row_in_block + 8 * i > k + 1, new, w[i]) if 8 * i < k + 2 else new
    w = jnp.concatenate(w, 0)
    diagonal = jnp.sum(jnp.where(lane == row, w, 0.0), 1, keepdims=True)
    left = jnp.sum(jnp.where(lane == row - 1, w, 0.0), 1, keepdims=True)
    odd = row % 2 == 1
    up = pltpu.roll(w, 1, 0)
    up_diagonal = pltpu.roll(jnp.broadcast_to(diagonal, (64, LANES)), 1, 0)
    ratio = jnp.where(odd, left / jnp.where(odd, up_diagonal, 1.0), 0.0)
    pivot = diagonal - ratio * left
    scaled = (w - ratio * up) * lax.rsqrt(pivot)
    return scaled[:, 64:]


def residual_kernel(total_dofs, gram, basis, image, classes, levels, out, ritz_ref, density):
    rows = band_densities(classes, levels, density)
    stiff, mass = unpacked(gram[...] * (1.0 / total_dofs))
    inverse = inverse_factor(mass)
    ritz = dot(dot(inverse, stiff, ((1,), (0,))), inverse, ((1,), (1,)))
    ritz_ref[...] = ritz
    mixed = dot(ritz, inverse, ((0,), (0,)))
    high, low = halves(jnp.concatenate([inverse, -mixed], 1))
    weights = jnp.concatenate([high, low, high], 1)
    for q in range(9):
        for c in range(3):
            t = c * 9 + q
            b = basis[pl.ds(t, 64, stride=27), :]
            v = image[pl.ds(t, 64, stride=27), :]
            x_high, x_low = halves(jnp.concatenate([v, b * rows[q]], 0))
            out[pl.ds(t, 64, stride=27), :] = lax.dot_general(
                weights,
                jnp.concatenate([x_high, x_high, x_low], 0),
                (((1,), (0,)), ((), ())),
                preferred_element_type=jnp.float32,
            )


def join_kernel(x_ref, out_ref):
    def piece(p, carry):
        for c in range(3):
            for q in range(9):
                out_ref[pl.ds(c * 72 + p * 9 + q, 8, stride=216), :] = x_ref[
                    pl.ds(p * 216 + c * 9 + q, 8, stride=27), :
                ]
        return carry

    lax.fori_loop(0, 8, piece, 0)


def room(mib):
    return pltpu.CompilerParams(vmem_limit_bytes=mib << 20)


def f32(*shape):
    return jax.ShapeDtypeStruct(shape, jnp.float32)


def total_sum(x):
    layer_axes = ("mesh_0", "modes_0", "modes_1")
    x = jnp.sum(lax.all_to_all(x, layer_axes, split_axis=0, concat_axis=0, tiled=True), 0)
    x = x + lax.ppermute(x, "mesh_2", [(0, 1), (1, 0)])
    x = jnp.broadcast_to(x[None], (8, *x.shape))
    return jnp.sum(lax.all_to_all(x, "mesh_1", split_axis=0, concat_axis=0, tiled=True), 0)


def per_device(subspace, classes, level_density):
    total_dofs = 3 * NX * NY * subspace.shape[2] * lax.axis_size(MESH)
    flat = subspace.reshape(1728, LANES)
    classes = classes.reshape(72, LANES)
    below = shifted(flat, MESH, 1)
    above = shifted(flat, MESH, -1)
    classes_up = shifted(classes, MESH, -1)
    split = pl.pallas_call(
        split_kernel,
        in_specs=[HBM],
        out_specs=HBM,
        out_shape=f32(1728, LANES),
        scratch_shapes=[
            pltpu.VMEM((3, 8, 72, LANES), jnp.float32),
            pltpu.VMEM((1728, LANES), jnp.float32),
            pltpu.SemaphoreType.DMA((3,)),
            pltpu.SemaphoreType.DMA((8,)),
        ],
        compiler_params=room(4),
        cost_estimate=pl.CostEstimate(flops=10**5, bytes_accessed=1_800_000, transcendentals=0),
        name="split",
    )
    pieces = split(pltpu.with_memory_space_constraint(flat.reshape(8, 3, 72, LANES), pltpu.HBM))

    def all_to_all(x):
        x = x.reshape(8, 216, LANES)
        return lax.all_to_all(x, MODES, split_axis=0, concat_axis=0, tiled=True).reshape(1728, LANES)

    basis = all_to_all(pieces)
    image_pieces = pl.pallas_call(
        stiffness_kernel,
        in_specs=[VMEM] * 5 + [SMEM],
        out_specs=VMEM,
        out_shape=f32(1728, LANES),
        scratch_shapes=[pltpu.VMEM((72, LANES), jnp.float32)] * 2
        + [pltpu.VMEM((2, n, 8, LANES), jnp.float32) for n in (108, 108, 108, 72, 36)],
        compiler_params=room(12),
        cost_estimate=pl.CostEstimate(
            flops=27_000_000, bytes_accessed=3_600_000, transcendentals=0
        ),
        name="stiffness",
    )(
        pltpu.with_memory_space_constraint(flat, pltpu.HBM),
        below,
        above,
        pltpu.with_memory_space_constraint(classes, pltpu.HBM),
        classes_up,
        level_density,
    )
    image = all_to_all(image_pieces)
    local = pl.pallas_call(
        gram_kernel,
        in_specs=[VMEM] * 3 + [SMEM],
        out_specs=VMEM,
        out_shape=f32(16, 40, LANES),
        scratch_shapes=[pltpu.VMEM((72, LANES), jnp.float32)],
        compiler_params=room(12),
        name="grams",
    )(basis, image, classes, level_density)
    gram = total_sum(local)
    residual_pieces, ritz_matrix = pl.pallas_call(
        functools.partial(residual_kernel, total_dofs),
        in_specs=[VMEM] * 4 + [SMEM],
        out_specs=[VMEM, VMEM],
        out_shape=[f32(1728, LANES), f32(64, 64)],
        scratch_shapes=[pltpu.VMEM((72, LANES), jnp.float32)],
        compiler_params=room(12),
        name="residual",
    )(gram, basis, image, classes, level_density)
    joined = pl.pallas_call(
        join_kernel,
        in_specs=[VMEM],
        out_specs=VMEM,
        out_shape=f32(1728, LANES),
        compiler_params=room(8),
        name="join",
    )(all_to_all(residual_pieces))
    return (joined.reshape(subspace.shape), ritz_matrix)


def solution(mesh):
    split = Mesh(
        mesh.devices.reshape(2, 8, 2, 2, 4), ("mesh_0", "mesh_1", "mesh_2", "modes_0", "modes_1")
    )
    placed = (P(MODES, None, MESH, None), P(MESH, None), P())
    return jax.shard_map(
        per_device,
        mesh=split,
        in_specs=placed,
        out_specs=(P(MODES, None, MESH, None), P()),
        check_vma=False,
    )
```
